512 devices in a mesh: tile: 64 (over y, x, core), own: 8 (over z).
Axes of the slice: x: 4, y: 8, z: 8, core: 2. Of those that a mesh axis runs over, the one named last changes fastest.
Arguments:
- features: bfloat16 [2048, 8, 768], P('tile'), may hold values from -6 to 6
- cotangent: bfloat16 [2048, 8, 768], P('tile'), may hold values from -6 to 6
- depth_kernel: float32 [7, 7, 768], replicated, may hold values from -0.875 to 0.875
- ln_gain: float32 [768], replicated, may hold values from 0.1 to 1.9
- weight_up: bfloat16 [768, 3072], P('tile', 'own'), may hold values from -0.21875 to 0.21875
- bias_up: float32 [3072], P('own'), may hold values from -3 to 3
- weight_down: bfloat16 [3072, 768], P('own', 'tile'), may hold values from -0.109375 to 0.109375
- layer_scale: float32 [768], replicated, may hold values from 0.3 to 3
- tissue: int32 [256, 1], P('tile'), may hold values 0 or 1
- lengths: int32 [64], replicated, may hold values from 1 to 4, 128 in all
Outputs:
- block_out: bfloat16 [2048, 8, 768], P(('tile', 'own'))
- grad_features: bfloat16 [2048, 8, 768], P(('tile', 'own'))
- muon_up: float32 [768, 3072], P('tile', 'own')
- muon_down: float32 [3072, 768], P('own', 'tile')
The draws below stay inside these ranges and needn't reach their ends.
Inputs may be any that keep to these rules, and one draw needn't show every extreme that they name: `lengths`: patch rows of slide in each strip; they sum to 128, and some strip has exactly 4.
All inputs are finite; a program needn't handle non-finite values. No bound on the sum of `tissue` on one device may be relied on, other than what follows from the above.
Results may differ from the reference program's by a relative error of at most 0.015.
Values may be sent and summed in bfloat16 or wider, within the bound.
A program may use at most 64 MiB of HBM per device.

```python
import math
import jax
import jax.numpy as jnp
import numpy as np
from jax import lax

D = 768
FF = 3072
KERNEL = 7
PATCH = 8
COLS = 8
P_AVG = 2
ITERS_NS = 2
P_MOST = 4
TILE_ROWS = 32
ROWS = 2048
PATCH_ROWS = 256
IMG_ROWS = 1024
MUON_COLS = 384
N_TILE = 64
N_OWN = 8


def plant(entries, stream_key, smallest, top_value):
    spot = [jax.random.randint(jax.random.fold_in(stream_key, axis), (), 0, length) for axis, length in enumerate(entries.shape)]
    widest = entries.shape.index(max(entries.shape))
    beside = spot[:widest] + [(spot[widest] + 1) % entries.shape[widest]] + spot[widest + 1:]
    return entries.at[tuple(spot)].set(smallest).at[tuple(beside)].set(top_value)


def shard_levels(rng, shape, shards, low, top_value):
    def one(position, blocks):
        heights = jax.random.uniform(jax.random.fold_in(jax.random.fold_in(rng, 6), position), (blocks,), jnp.float32, low / len(shards), top_value / len(shards))
        return jnp.repeat(jnp.exp(heights), shape[position] // blocks).reshape((-1,) + (1,) * (len(shape) - position - 1))

    level = one(*shards[0])
    for cut in shards[1:]:
        level = level * one(*cut)
    return level


def split_up(amount, total, bound, lean):
    portions = [(1 << 20) // math.isqrt(rank ** lean) + 1 for rank in range(2, amount + 1)]
    spare, holding = total - bound - (amount - 1), [1] * (amount - 1)
    while spare > 0:
        free = [i for i in range(amount - 1) if holding[i] < bound]
        whole, left = sum([portions[i] for i in free]), spare
        for i in free:
            more = min(bound - holding[i], max(1, left * portions[i] // whole), spare)
            holding[i] = holding[i] + more
            spare = spare - more
    return np.array([bound] + holding)


def ragged_sizes(rng, count, total, bound, lean):
    if count == 2:
        one = jax.random.randint(rng, (), max(1, total - bound), min(bound, total - 1) + 1)
        return jnp.stack([one, total - one])
    tallies = jnp.asarray(split_up(count, total, bound, lean), jnp.int32)
    pairs = (count - 1) // 2
    giver, taker = tallies[1:1 + 2 * pairs:2], tallies[2:2 + 2 * pairs:2]
    slack = jnp.minimum(giver - 1, bound - taker)
    passed = jax.random.randint(jax.random.fold_in(rng, 1), (pairs,), 0, 1 << 20) % (slack + 1)
    tallies = tallies.at[1:1 + 2 * pairs:2].set(giver - passed).at[2:2 + 2 * pairs:2].set(taker + passed)
    return tallies[jax.random.permutation(jax.random.fold_in(rng, 2), count)]


def gaussian(stream_key, extent, width, limit, split=(), held_as=jnp.bfloat16):
    entries = width * jax.random.normal(stream_key, extent, jnp.float32)
    if split:
        entries = entries * shard_levels(stream_key, extent, split, -0.22, 0.18)
    return jnp.clip(entries, -limit, limit).astype(held_as)


def setup_inputs(seed: int = 0) -> dict:
    streams_of = jax.random.split(jax.random.key(seed), 11)
    return {
        "features": gaussian(streams_of[0], (ROWS, COLS, D), 1.0, 6.0, ((0, 64),)),
        "cotangent": gaussian(streams_of[1], (ROWS, COLS, D), 1.0, 6.0, ((0, 64),)),
        "depth_kernel": gaussian(streams_of[2], (KERNEL, KERNEL, D), (KERNEL * KERNEL) ** -0.5, 0.875, (), jnp.float32),
        "ln_gain": jnp.clip(1.0 + 0.18 * jax.random.normal(streams_of[3], (D,), jnp.float32), 0.1, 1.9),
        "weight_up": gaussian(streams_of[4], (D, FF), D ** -0.5, 0.21875, ((0, 64), (1, 8))),
        "bias_up": gaussian(streams_of[5], (FF,), 0.5, 3.0, ((0, 8),), jnp.float32),
        "weight_down": gaussian(streams_of[6], (FF, D), FF ** -0.5, 0.109375, ((0, 8), (1, 64))),
        "layer_scale": jnp.clip(jnp.exp(jax.random.uniform(streams_of[7], (D,), jnp.float32, math.log(0.3), math.log(3.0))), 0.3, 3.0),
        "tissue": plant((jax.random.randint(streams_of[8], (PATCH_ROWS, COLS // PATCH), 0, 4) < 3).astype(jnp.int32), jax.random.fold_in(streams_of[8], 1), 0, 1),
        "lengths": ragged_sizes(streams_of[9], N_TILE, N_TILE * P_AVG, P_MOST, 2).astype(jnp.int32),
    }


INV_ROOT_TWO = 0.7071067811865476
INV_ROOT_TAU = 0.3989422804014327
NS_A = 3.4445
NS_B = -4.775
NS_C = 2.0315
EPS_NORM = 1e-06
HIGHEST_PREC = lax.Precision.HIGHEST

def gelu_exact(hidden):
    return 0.5 * hidden * (1.0 + lax.erf(hidden * INV_ROOT_TWO))

def gelu_slope(hidden):
    return 0.5 * (1.0 + lax.erf(hidden * INV_ROOT_TWO)) + hidden * jnp.exp(-0.5 * hidden * hidden) * INV_ROOT_TAU

def depthwise(framed, kernel):
    margin = kernel.shape[0] // 2
    padded = jnp.pad(framed, ((0, 0), (margin, margin), (0, 0)))
    row_count = framed.shape[0] - 2 * margin
    col_count = framed.shape[1]
    totals = jnp.zeros((row_count, col_count, framed.shape[2]), jnp.float32)
    for row_tap in range(kernel.shape[0]):
        for col_tap in range(kernel.shape[1]):
            totals = totals + kernel[row_tap, col_tap] * padded[row_tap:row_tap + row_count, col_tap:col_tap + col_count]
    return totals

def layer_norm(mixed, ln_gain):
    average = lax.optimization_barrier(jnp.mean(mixed, axis=-1, keepdims=True))
    shifted = mixed - average
    variance = lax.optimization_barrier(jnp.mean(shifted * shifted, axis=-1, keepdims=True))
    inv_std = lax.rsqrt(variance + 1e-06)
    centred = shifted * inv_std
    return (centred, inv_std, (centred * ln_gain).astype(jnp.bfloat16))

def norm_back(grad_normed, centred, inv_std, ln_gain):
    scaled_grad = grad_normed * ln_gain
    first_mean = lax.optimization_barrier(jnp.mean(scaled_grad, axis=-1, keepdims=True))
    second_mean = lax.optimization_barrier(jnp.mean(scaled_grad * centred, axis=-1, keepdims=True))
    return inv_std * (scaled_grad - first_mean - centred * second_mean)

def blockwise_sum(left, right, right_rows):
    block_width = left.shape[1] // N_OWN
    total = jnp.zeros((left.shape[0], right.shape[1] if right_rows else right.shape[0]), jnp.float32)
    for block_index in range(N_OWN):
        lo_col = block_index * block_width
        piece = left[:, lo_col:lo_col + block_width]
        if right_rows:
            term = jnp.dot(piece, right[lo_col:lo_col + block_width], preferred_element_type=jnp.float32)
        else:
            term = lax.dot_general(piece, right[:, lo_col:lo_col + block_width], (((1,), (1,)), ((), ())), preferred_element_type=jnp.float32)
        rounded = lax.optimization_barrier(term.astype(jnp.bfloat16))
        total = total + rounded.astype(jnp.float32)
    return total

def branch_pass(normed_rows, grad_branch, up_full, bias_up, down_full):
    hidden = jnp.dot(normed_rows, up_full, preferred_element_type=jnp.float32) + bias_up
    activation = gelu_exact(hidden).astype(jnp.bfloat16)
    branch = blockwise_sum(activation, down_full, True)
    grad_act = lax.dot_general(grad_branch, down_full, (((1,), (1,)), ((), ())), preferred_element_type=jnp.float32)
    grad_hidden = (grad_act * gelu_slope(hidden)).astype(jnp.bfloat16)
    grad_normed = blockwise_sum(grad_hidden, up_full, False)
    grad_up = lax.dot_general(normed_rows, grad_hidden, (((0,), (0,)), ((), ())), preferred_element_type=jnp.float32)
    grad_down_t = lax.dot_general(grad_branch, activation, (((0,), (0,)), ((), ())), preferred_element_type=jnp.float32)
    return (branch, grad_normed, grad_up, grad_down_t)

def ns_update(block, gram_matrix):
    polynomial = NS_B * gram_matrix + NS_C * jnp.dot(gram_matrix, gram_matrix, precision=HIGHEST_PREC, preferred_element_type=jnp.float32)
    return NS_A * block + jnp.dot(block, polynomial, precision=HIGHEST_PREC, preferred_element_type=jnp.float32)

def newton_schulz(gradient):
    scaled = gradient * lax.rsqrt(jnp.sum(gradient * gradient) + EPS_NORM)
    for sweep_index in range(ITERS_NS):
        gram_matrix = lax.dot_general(scaled, scaled, (((0,), (0,)), ((), ())), precision=HIGHEST_PREC, preferred_element_type=jnp.float32)
        scaled = ns_update(scaled, gram_matrix)
    return scaled

def reference(features, cotangent, depth_kernel, ln_gain, weight_up, bias_up, weight_down, layer_scale, tissue, lengths):
    margin = KERNEL // 2
    row_counts = (PATCH * lengths).astype(jnp.int32)
    row_starts = (jnp.cumsum(row_counts) - row_counts).astype(jnp.int32)
    buffer_row = jnp.arange(ROWS, dtype=jnp.int32)
    strip_owner = buffer_row // TILE_ROWS
    inner_row = buffer_row % TILE_ROWS
    row_live = inner_row < row_counts[strip_owner]
    target = jnp.where(row_live, row_starts[strip_owner] + inner_row, IMG_ROWS).astype(jnp.int32)
    source = jnp.minimum(target, IMG_ROWS - 1).astype(jnp.int32)
    patch_mask = jnp.repeat(jnp.repeat(tissue, PATCH, axis=0), PATCH, axis=1)

    def place(buffer_field):
        blank_field = jnp.zeros((IMG_ROWS,) + buffer_field.shape[1:], buffer_field.dtype)
        return blank_field.at[target].set(buffer_field, mode='drop')

    def pick(image_field):
        return jnp.where(row_live[:, None, None], image_field[source], jnp.zeros((), image_field.dtype))
    image = place(features).astype(jnp.float32)
    cot_image = place(cotangent).astype(jnp.float32)
    keep_mask = place(patch_mask).astype(jnp.float32)[:, :, None]
    mixed = depthwise(jnp.pad(image, ((margin, margin), (0, 0), (0, 0))), depth_kernel)
    centred, inv_std, normed = layer_norm(mixed, ln_gain)
    grad_branch = (keep_mask * layer_scale * cot_image).astype(jnp.bfloat16)
    branch, grad_normed, grad_up, grad_down_t = branch_pass(normed.reshape(-1, D), grad_branch.reshape(-1, D), weight_up, bias_up, weight_down)
    out_image = (image + keep_mask * layer_scale * branch.reshape(image.shape)).astype(jnp.bfloat16)
    grad_mixed = norm_back(grad_normed.reshape(image.shape), centred, inv_std, ln_gain)
    spread = depthwise(jnp.pad(grad_mixed, ((margin, margin), (0, 0), (0, 0))), depth_kernel[::-1, ::-1])
    grad_image = (cot_image + spread).astype(jnp.bfloat16)
    blocks_up = grad_up.reshape(D, N_OWN, MUON_COLS).transpose(1, 0, 2)
    blocks_down = grad_down_t.reshape(D, N_OWN, MUON_COLS).transpose(1, 0, 2)
    ortho_up = lax.map(newton_schulz, blocks_up).transpose(1, 0, 2).reshape(D, FF)
    ortho_down = lax.map(newton_schulz, blocks_down).transpose(1, 0, 2).reshape(D, FF)
    return (pick(out_image), pick(grad_image), ortho_up, ortho_down.T)
```

```python
import jax
import jax.numpy as jnp
from jax import lax
from jax.experimental import pallas as pl
from jax.experimental.pallas import tpu as pltpu
from jax.sharding import PartitionSpec as P

MESH = pl.DeviceIdType.MESH
F32 = jnp.float32
BF16 = jnp.bfloat16

NY, NX, NZ = 8, 4, 8
NT = NY * NX * 2
D = 768
HID = 384
TOK = 256
CH = D // 128
RB = 24
OWN_TOK = 32

INV_ROOT_TWO = 0.7071067811865476
INV_ROOT_TAU = 0.3989422804014327
NS_A = 3.4445
NS_B = -4.775
NS_C = 2.0315
EPS_NORM = 1e-06
HIGH = lax.Precision.HIGH


def f32dot(a, b, dims=(((1,), (0,)), ((), ()))):
    return lax.dot_general(a, b, dims, precision=HIGH, preferred_element_type=F32)


def bdot(a, b, dims=(((1,), (0,)), ((), ()))):
    return lax.dot_general(a, b, dims, preferred_element_type=F32)


NT_DIMS = (((1,), (1,)), ((), ()))
TN_DIMS = (((0,), (0,)), ((), ()))


def body(
    lens, tissue, feat, cot, dk, gain, wu, bias, wd, scale,
    out_ref, gout_ref, mu_ref, md_ref,
    pieces, piece_in, t24, wg, wm, fx, rim, halo, frame, mixed, inv_s, left, right,
    zs, zr, bs, br, gs, grv, gf, gb, rx, gx, ty, ry, grow, ga, gm16, hg, nb, ct, chd, frame2, xo,
    ss, rs,
):
    t = lax.axis_index("tile")
    o = lax.axis_index("own")
    c = lax.rem(t, 2)
    chip = t // 2
    x = lax.rem(chip, NX)
    y = chip // NX
    sib = t + 1 - 2 * c

    def tile_at(yy, xx):
        return (yy * NX + xx) * 2 + c

    counter = [0]
    sent = []

    def sem_ids(n):
        first = counter[0]
        counter[0] += n
        return first

    def copy(src, dst, sem, dev):
        return pltpu.make_async_remote_copy(
            src_ref=src, dst_ref=dst, send_sem=ss.at[sem], recv_sem=rs.at[sem],
            device_id=dev, device_id_type=MESH,
        )

    def send(src, dst, sem, dev):
        cp = copy(src, dst, sem, dev)
        cp.start()
        sent.append(cp)

    def arrived(dst, sem):
        copy(dst, dst, sem, (t, o)).wait_recv()

    bar = pltpu.get_barrier_semaphore()

    def greet(dev):
        pl.semaphore_signal(bar, inc=1, device_id=dev, device_id_type=MESH)

    up_t = lax.rem(t + 1, NT)
    dn_t = lax.rem(t + NT - 1, NT)
    greet((sib, o))
    for k in range(1, NY):
        greet((tile_at(lax.rem(y + k, NY), x), o))
    for k in range(1, NX):
        greet((tile_at(y, lax.rem(x + k, NX)), o))
    for k in range(1, NZ):
        greet((t, lax.rem(o + k, NZ)))
    greet((up_t, o))
    greet((dn_t, o))
    first_own = o == 0
    odd_own = lax.rem(o, 2) == 1

    @pl.when(first_own)
    def _():
        for q in range(4):
            greet((dn_t, 2 * q + 1))

    @pl.when(odd_own)
    def _():
        greet((up_t, 0))

    length = lens[t]

    pieces[0] = wu[...]
    pieces[1] = wd[...]
    rim[0] = feat[0:24, :].astype(F32).astype(BF16)
    tail = feat[0:64, :].astype(F32)[40:64]
    for q in range(1, 4):
        tail = jnp.where(length == q + 1, feat[64 * q : 64 * q + 64, :].astype(F32)[40:64], tail)
    rim[1] = tail.astype(BF16)

    expected = 1 + (NY - 1) + (NX - 1) + (NZ - 1) + 2
    pl.semaphore_wait(bar, expected + 4 * ((NZ - o) // NZ) + lax.rem(o, 2))

    s_piece = sem_ids(1)
    send(pieces.at[1 - c], piece_in, s_piece, (sib, o))
    s_halo = sem_ids(2)
    send(rim.at[1], halo.at[0], s_halo, (up_t, o))
    send(rim.at[0], halo.at[1], s_halo + 1, (dn_t, o))

    frame[...] = jnp.zeros_like(frame)
    for q in range(4):
        rows = slice(64 * q, 64 * q + 64)
        live = length > q
        keep = jnp.where(live, tissue[q, 0], 0).astype(F32)
        f = feat[rows, :].astype(F32)
        if q:
            f = jnp.where(live, f, 0.0)
        for ch in range(CH):
            frame[ch, 3 + 8 * q : 11 + 8 * q, 3:11, :] = f[:, 128 * ch : 128 * ch + 128].reshape(8, 8, 128)
        left[1, rows, :] = ((keep * scale[...]) * cot[rows, :].astype(F32)).astype(BF16)

    arrived(piece_in, s_piece)
    mine = pieces[c].astype(F32)
    other = piece_in[...].astype(F32)
    t24[0:12, :] = jnp.where(c == 0, mine, other)
    t24[12:24, :] = jnp.where(c == 0, other, mine)
    wg[c, y, x] = t24[...].astype(BF16)

    def gather_y(buf, s0):
        for k in range(1, NY):
            send(buf.at[y, x], buf.at[y, x], s0 + k - 1, (tile_at(lax.rem(y + k, NY), x), o))

    def gather_y_wait(buf, s0):
        for k in range(1, NY):
            arrived(buf.at[lax.rem(y + NY - k, NY), x], s0 + k - 1)

    def gather_x(buf, s0):
        for k in range(1, NX):
            send(buf.at[:, x], buf.at[:, x], s0 + k - 1, (tile_at(y, lax.rem(x + k, NX)), o))

    s_wy = sem_ids(NY - 1)
    s_wx = sem_ids(NX - 1)
    s_ws = sem_ids(NX)
    wg_c = wg.at[c]
    gather_y(wg_c, s_wy)

    arrived(halo.at[0], s_halo)
    arrived(halo.at[1], s_halo + 1)
    before = jnp.where(t > 0, halo[0].astype(F32), 0.0)
    after = jnp.where(t < NT - 1, halo[1].astype(F32), 0.0)
    for ch in range(CH):
        lanes = slice(128 * ch, 128 * ch + 128)
        frame[ch, 0:3, 3:11, :] = before[:, lanes].reshape(3, 8, 128)
        nxt = after[:, lanes].reshape(3, 8, 128)
        for q in range(1, 4):
            old = frame[ch, 3 + 8 * q : 6 + 8 * q, 3:11, :]
            frame[ch, 3 + 8 * q : 6 + 8 * q, 3:11, :] = jnp.where(length == q, nxt, old)
        frame[ch, 35:38, 3:11, :] = jnp.where(length == 4, nxt, 0.0)

    def conv_half(h):
        def chunk(ch, _):
            lanes = pl.ds(pl.multiple_of(ch * 128, 128), 128)
            acc = jnp.zeros((16, 8, 128), F32)
            for i in range(7):
                for j in range(7):
                    w = dk[i, j : j + 1, lanes].reshape(1, 1, 128)
                    acc = acc + w * frame[ch, 16 * h + i : 16 * h + i + 16, j : j + 8, :]
            mixed[128 * h : 128 * h + 128, lanes] = acc.reshape(128, 128)
            return 0

        lax.fori_loop(0, CH, chunk, 0)

    conv_half(0)
    gather_y_wait(wg_c, s_wy)
    gather_x(wg_c, s_wx)
    send(wg_c.at[:, x], wg_c.at[:, x], s_ws, (sib, o))
    conv_half(1)

    for q in range(4):
        rows = slice(64 * q, 64 * q + 64)
        m = mixed[rows, :]
        shifted = m - jnp.sum(m, axis=-1, keepdims=True) * (1.0 / D)
        var = jnp.sum(shifted * shifted, axis=-1, keepdims=True) * (1.0 / D)
        inv = lax.rsqrt(var + 1e-06)
        centred = shifted * inv
        mixed[rows, :] = centred
        inv_s[rows, :] = inv
        left[0, rows, :] = (centred * gain[...]).astype(BF16)

    for k in range(1, NX):
        col = lax.rem(x + NX - k, NX)
        arrived(wg_c.at[:, col], s_wx + k - 1)
        send(wg_c.at[:, col], wg_c.at[:, col], s_ws + k, (sib, o))
    wm[c] = wg[c].astype(F32).reshape(D, HID).astype(BF16)
    wg_o = wg.at[1 - c]
    for k in range(NX):
        arrived(wg_o.at[:, lax.rem(x + NX - k, NX)], s_ws + k)
    wm[1 - c] = wg[1 - c].astype(F32).reshape(D, HID).astype(BF16)

    up_w = wm[0]
    down_w = wm[1]
    hidden = bdot(left[0], up_w) + bias[...]
    phi = 0.5 * (1.0 + lax.erf(hidden * INV_ROOT_TWO))
    right[1] = (hidden * phi).astype(BF16)
    grad_act = bdot(left[1], down_w)
    slope = phi + hidden * jnp.exp(-0.5 * hidden * hidden) * INV_ROOT_TAU
    right[0] = (grad_act * slope).astype(BF16)

    s_g = sem_ids(1)
    gs[...] = bdot(left[1 - c], right[1 - c], TN_DIMS).reshape(NY, NX, RB, HID).astype(BF16)
    send(gs, grv, s_g, (sib, o))

    def scatter_z(value, buf, slots, s0):
        buf[...] = value.reshape(NZ, OWN_TOK, D).astype(BF16)
        for k in range(1, NZ):
            dest = lax.rem(o + k, NZ)
            send(buf.at[dest], slots.at[k - 1], s0 + k - 1, (t, dest))

    def scatter_z_sum(buf, slots, s0):
        total = buf[o].astype(F32)
        for k in range(1, NZ):
            arrived(slots.at[k - 1], s0 + k - 1)
            total = total + slots[k - 1].astype(F32)
        return total

    s_z = sem_ids(NZ - 1)
    s_b = sem_ids(NZ - 1)
    scatter_z(bdot(right[0], up_w, NT_DIMS), zs, zr, s_z)
    gf[...] = bdot(left[c], right[c], TN_DIMS).reshape(NY, NX, RB, HID)

    arrived(grv, s_g)
    pair = gf[...] + grv[...].astype(F32)
    gf[...] = pair
    gb[...] = pair.astype(BF16)
    s_rx = sem_ids(NX - 1)
    for k in range(1, NX):
        col = lax.rem(x + k, NX)
        send(gb.at[:, col], rx.at[k - 1], s_rx + k - 1, (tile_at(y, col), o))
    scatter_z(bdot(right[1], down_w, NT_DIMS), bs, br, s_b)

    for k in range(1, NX):
        arrived(rx.at[k - 1], s_rx + k - 1)
    xsum = gf[:, x] + rx[0].astype(F32) + rx[1].astype(F32) + rx[2].astype(F32)
    gx[...] = xsum
    ty[...] = xsum.astype(BF16)
    s_ry = sem_ids(NY - 1)
    for k in range(1, NY):
        row = lax.rem(y + k, NY)
        send(ty.at[row], ry.at[k - 1], s_ry + k - 1, (tile_at(row, x), o))

    grad_normed = scatter_z_sum(zs, zr, s_z)
    own_rows = pl.ds(pl.multiple_of(o * OWN_TOK, OWN_TOK), OWN_TOK)
    own_live = length > o // 2
    centred = mixed[own_rows, :]
    g = grad_normed * gain[...]
    mean1 = jnp.sum(g, axis=-1, keepdims=True) * (1.0 / D)
    mean2 = jnp.sum(g * centred, axis=-1, keepdims=True) * (1.0 / D)
    grad_mixed = inv_s[own_rows, :] * (g - mean1 - centred * mean2)
    grad_mixed = jnp.where(own_live, grad_mixed, 0.0)
    hg[...] = grad_mixed.astype(BF16)
    s_h = sem_ids(2)
    s_ct = sem_ids(4)
    s_ch = sem_ids(1)
    send(hg, nb.at[0], s_h, (t, lax.rem(o + 1, NZ)))
    send(hg, nb.at[1], s_h + 1, (t, lax.rem(o + NZ - 1, NZ)))
    s_c4 = sem_ids(4)

    @pl.when(first_own)
    def _():
        for q in range(4):
            pltpu.make_async_remote_copy(
                src_ref=hg, dst_ref=chd, send_sem=ss.at[s_c4 + q], recv_sem=rs.at[s_ch],
                device_id=(dn_t, 2 * q + 1), device_id_type=MESH,
            ).start()

    @pl.when(odd_own)
    def _():
        q = o // 2
        pltpu.make_async_remote_copy(
            src_ref=hg, dst_ref=ct.at[q], send_sem=ss.at[s_c4], recv_sem=rs.at[s_ct + q],
            device_id=(up_t, 0), device_id_type=MESH,
        ).start()

    frame2[...] = jnp.zeros_like(frame2)
    for ch in range(CH):
        frame2[ch, 3:7, 3:11, :] = grad_mixed[:, 128 * ch : 128 * ch + 128].reshape(4, 8, 128)

    for k in range(1, NY):
        arrived(ry.at[k - 1], s_ry + k - 1)
    total = gx[y]
    for k in range(1, NY):
        total = total + ry[k - 1].astype(F32)
    grow[...] = total
    ga[y, x] = total.astype(BF16)
    s_gy = sem_ids(NY - 1)
    s_gx = sem_ids(NX - 1)
    gather_y(ga, s_gy)

    def put_before(block):
        rows3 = block.astype(F32)[8:32]
        for ch in range(CH):
            frame2[ch, 0:3, 3:11, :] = rows3[:, 128 * ch : 128 * ch + 128].reshape(3, 8, 128)

    def put_after(block):
        rows3 = block.astype(F32)[0:24]
        for ch in range(CH):
            frame2[ch, 7:10, 3:11, :] = rows3[:, 128 * ch : 128 * ch + 128].reshape(3, 8, 128)

    arrived(nb.at[0], s_h)
    arrived(nb.at[1], s_h + 1)

    @pl.when(first_own)
    def _():
        for q in range(4):
            arrived(ct.at[q], s_ct + q)
        prev_len = lens[dn_t]
        block = ct[0].astype(F32)
        for q in range(1, 4):
            block = jnp.where(prev_len == q + 1, ct[q].astype(F32), block)
        put_before(jnp.where(t > 0, block, 0.0))
        for q in range(4):
            pltpu.make_async_remote_copy(
                src_ref=hg, dst_ref=chd, send_sem=ss.at[s_c4 + q], recv_sem=rs.at[s_ch],
                device_id=(dn_t, 2 * q + 1), device_id_type=MESH,
            ).wait_send()

    @pl.when(jnp.logical_not(first_own))
    def _():
        put_before(nb[0])

    @pl.when(odd_own)
    def _():
        arrived(chd, s_ch)
        q = o // 2
        edge = jnp.where(t < NT - 1, chd[...].astype(F32), 0.0)
        put_after(jnp.where(length == q + 1, edge, nb[1].astype(F32)))
        pltpu.make_async_remote_copy(
            src_ref=hg, dst_ref=ct.at[q], send_sem=ss.at[s_c4], recv_sem=rs.at[s_ct + q],
            device_id=(up_t, 0), device_id_type=MESH,
        ).wait_send()

    @pl.when(jnp.logical_not(odd_own))
    def _():
        put_after(nb[1])

    def chunk2(ch, _):
        lanes = pl.ds(pl.multiple_of(ch * 128, 128), 128)
        acc = jnp.zeros((4, 8, 128), F32)
        for i in range(7):
            for j in range(7):
                w = dk[6 - i, 6 - j : 7 - j, lanes].reshape(1, 1, 128)
                acc = acc + w * frame2[ch, i : i + 4, j : j + 8, :]
        res = cot[own_rows, lanes].astype(F32) + acc.reshape(OWN_TOK, 128)
        gout_ref[:, lanes] = jnp.where(own_live, res, 0.0).astype(BF16)
        return 0

    lax.fori_loop(0, CH, chunk2, 0)

    gather_y_wait(ga, s_gy)
    gather_x(ga, s_gx)

    branch = scatter_z_sum(bs, br, s_b)
    own_keep = jnp.where(own_live, tissue[o // 2, 0], 0).astype(F32)
    res = feat[own_rows, :].astype(F32) + (own_keep * scale[...]) * branch
    out_ref[...] = jnp.where(own_live, res, 0.0).astype(BF16)

    for k in range(1, NX):
        arrived(ga.at[:, lax.rem(x + NX - k, NX)], s_gx + k - 1)

    whole = ga[...].astype(F32).reshape(D, HID)
    norm2 = jnp.sum(jnp.sum(whole * whole, axis=0, keepdims=True), axis=1, keepdims=True)
    root = lax.rsqrt(norm2 + EPS_NORM)
    gm16[...] = whole.astype(BF16)
    g16 = gm16[...]
    gram = bdot(g16, g16, TN_DIMS) * (root * root)
    eye = (
        lax.broadcasted_iota(jnp.int32, (HID, HID), 0) == lax.broadcasted_iota(jnp.int32, (HID, HID), 1)
    ).astype(F32)

    def poly(a):
        return NS_A * eye + NS_B * a + NS_C * f32dot(a, a)

    p0 = poly(gram)
    gram1 = f32dot(f32dot(gram, p0), p0)
    p1 = poly(gram1)
    xo[c] = f32dot(f32dot(grow[...] * root, p0), p1)
    s_x = sem_ids(1)
    send(xo.at[c], xo.at[c], s_x, (sib, o))
    arrived(xo.at[1 - c], s_x)
    mu_ref[...] = jnp.where(c == 0, xo[0, 0:12, :], xo[0, 12:24, :])
    md_ref[...] = jnp.where(c == 0, xo[1, 0:12, :], xo[1, 12:24, :])

    for cp in sent:
        cp.wait_send()


SEMS = 96


def shards(features, cotangent, depth_kernel, ln_gain, weight_up, bias_up, weight_down, layer_scale, tissue, lengths):
    vmem = pl.BlockSpec(memory_space=pltpu.VMEM)
    smem = pl.BlockSpec(memory_space=pltpu.SMEM)
    block4 = (NY, NX, RB, HID)
    scratch = [
        pltpu.VMEM((2, 12, HID), BF16),
        pltpu.VMEM((12, HID), BF16),
        pltpu.VMEM((24, HID), F32),
        pltpu.VMEM((2,) + block4, BF16),
        pltpu.VMEM((2, D, HID), BF16),
        pltpu.VMEM((8, 128), F32),
        pltpu.VMEM((2, 24, D), BF16),
        pltpu.VMEM((2, 24, D), BF16),
        pltpu.VMEM((CH, 38, 16, 128), F32),
        pltpu.VMEM((TOK, D), F32),
        pltpu.VMEM((TOK, 1), F32),
        pltpu.VMEM((2, TOK, D), BF16),
        pltpu.VMEM((2, TOK, HID), BF16),
        pltpu.VMEM((NZ, OWN_TOK, D), BF16),
        pltpu.VMEM((NZ - 1, OWN_TOK, D), BF16),
        pltpu.VMEM((NZ, OWN_TOK, D), BF16),
        pltpu.VMEM((NZ - 1, OWN_TOK, D), BF16),
        pltpu.VMEM(block4, BF16),
        pltpu.VMEM(block4, BF16),
        pltpu.VMEM(block4, F32),
        pltpu.VMEM(block4, BF16),
        pltpu.VMEM((NX - 1, NY, RB, HID), BF16),
        pltpu.VMEM((NY, RB, HID), F32),
        pltpu.VMEM((NY, RB, HID), BF16),
        pltpu.VMEM((NY - 1, RB, HID), BF16),
        pltpu.VMEM((RB, HID), F32),
        pltpu.VMEM(block4, BF16),
        pltpu.VMEM((D, HID), BF16),
        pltpu.VMEM((OWN_TOK, D), BF16),
        pltpu.VMEM((2, OWN_TOK, D), BF16),
        pltpu.VMEM((4, OWN_TOK, D), BF16),
        pltpu.VMEM((OWN_TOK, D), BF16),
        pltpu.VMEM((CH, 10, 16, 128), F32),
        pltpu.VMEM((2, RB, HID), F32),
        pltpu.SemaphoreType.DMA((SEMS,)),
        pltpu.SemaphoreType.DMA((SEMS,)),
    ]
    outs = pl.pallas_call(
        body,
        out_shape=(
            jax.ShapeDtypeStruct((OWN_TOK, D), BF16),
            jax.ShapeDtypeStruct((OWN_TOK, D), BF16),
            jax.ShapeDtypeStruct((12, HID), F32),
            jax.ShapeDtypeStruct((12, HID), F32),
        ),
        in_specs=[smem, smem] + [vmem] * 8,
        out_specs=(vmem,) * 4,
        scratch_shapes=scratch,
        compiler_params=pltpu.CompilerParams(
            collective_id=0, has_side_effects=True, vmem_limit_bytes=48 << 20
        ),
    )(
        lengths,
        tissue,
        features.reshape(TOK, D),
        cotangent.reshape(TOK, D),
        depth_kernel,
        ln_gain.reshape(1, D),
        weight_up,
        bias_up.reshape(1, HID),
        weight_down.T,
        layer_scale.reshape(1, D),
    )
    block_out, grad_features, muon_up, muon_down_t = outs
    return (
        block_out.reshape(4, 8, D),
        grad_features.reshape(4, 8, D),
        muon_up,
        muon_down_t.T,
    )


def solution(mesh):
    in_specs = (
        P("tile", None, None),
        P("tile", None, None),
        P(),
        P(),
        P("tile", "own"),
        P("own"),
        P("own", "tile"),
        P(),
        P("tile", None),
        P(),
    )
    out_specs = (
        P(("tile", "own"), None, None),
        P(("tile", "own"), None, None),
        P("tile", "own"),
        P("own", "tile"),
    )
    return jax.shard_map(shards, mesh=mesh, in_specs=in_specs, out_specs=out_specs, check_vma=False)
```

```python
import jax
import jax.numpy as jnp
from jax import lax
from jax.experimental import pallas as pl
from jax.experimental.pallas import tpu as pltpu
from jax.sharding import PartitionSpec as P

MESH = pl.DeviceIdType.MESH
F32 = jnp.float32
BF16 = jnp.bfloat16

NY, NX, NZ = 8, 4, 8
NT = NY * NX * 2
D = 768
HID = 384
TOK = 256
CH = D // 128
RB = 24
OWN_TOK = 32

INV_ROOT_TWO = 0.7071067811865476
INV_ROOT_TAU = 0.3989422804014327
NS_A = 3.4445
NS_B = -4.775
NS_C = 2.0315
EPS_NORM = 1e-06
HIGH = lax.Precision.HIGH


def f32dot(a, b, dims=(((1,), (0,)), ((), ()))):
    return lax.dot_general(a, b, dims, precision=HIGH, preferred_element_type=F32)


def bdot(a, b, dims=(((1,), (0,)), ((), ()))):
    return lax.dot_general(a, b, dims, preferred_element_type=F32)


NT_DIMS = (((1,), (1,)), ((), ()))
TN_DIMS = (((0,), (0,)), ((), ()))


def body(
    lens_h, tissue_h, feat_h, cot_h, dk_h, gain_h, wu_h, bias_h, wd_h, scale_h,
    out_ref, gout_ref, mu_ref, md_ref,
    lens, tissue, feat, cot, dk, gain1, bias1, scale1, pieces, piece_in, t24, wg, wm, rim, halo, frame, mixed, inv_s, left, right,
    zs, zr, bs, br, gs, grv, gf, gb, rx, ty, ry, grow, ga, gm16, hg, nb, ct, chd, frame2, xo,
    ss, rs, ls,
):
    t = lax.axis_index("tile")
    o = lax.axis_index("own")
    c = lax.rem(t, 2)
    chip = t // 2
    x = lax.rem(chip, NX)
    y = chip // NX
    sib = t + 1 - 2 * c

    def tile_at(yy, xx):
        return (yy * NX + xx) * 2 + c

    counter = [0]
    sent = []

    def sem_ids(n):
        first = counter[0]
        counter[0] += n
        return first

    def copy(src, dst, sem, dev):
        return pltpu.make_async_remote_copy(
            src_ref=src, dst_ref=dst, send_sem=ss.at[sem], recv_sem=rs.at[sem],
            device_id=dev, device_id_type=MESH,
        )

    def send(src, dst, sem, dev):
        cp = copy(src, dst, sem, dev)
        cp.start()
        sent.append(cp)

    def arrived(dst, sem):
        copy(dst, dst, sem, (t, o)).wait_recv()

    fetches = {}
    for n, (name, src, dst) in enumerate(
        (
            ("wu", wu_h, pieces.at[0]), ("wd", wd_h, pieces.at[1]), ("lens", lens_h, lens),
            ("feat", feat_h, feat), ("tissue", tissue_h, tissue), ("dk", dk_h, dk), ("gain", gain_h, gain1),
            ("scale", scale_h, scale1), ("cot", cot_h, cot), ("bias", bias_h, bias1),
        )
    ):
        fetches[name] = pltpu.make_async_copy(src, dst, ls.at[n])
        fetches[name].start()

    bar = pltpu.get_barrier_semaphore()

    def greet(dev):
        pl.semaphore_signal(bar, inc=1, device_id=dev, device_id_type=MESH)

    up_t = lax.rem(t + 1, NT)
    dn_t = lax.rem(t + NT - 1, NT)
    greet((sib, o))
    for k in range(1, NY):
        greet((tile_at(lax.rem(y + k, NY), x), o))
    for k in range(1, NX):
        greet((tile_at(y, lax.rem(x + k, NX)), o))
    for k in range(1, NZ):
        greet((t, lax.rem(o + k, NZ)))
    greet((up_t, o))
    greet((dn_t, o))
    first_own = o == 0
    odd_own = lax.rem(o, 2) == 1

    @pl.when(first_own)
    def _():
        for q in range(4):
            greet((dn_t, 2 * q + 1))

    @pl.when(odd_own)
    def _():
        greet((up_t, 0))

    expected = 1 + (NY - 1) + (NX - 1) + (NZ - 1) + 2
    fetches["wu"].wait()
    fetches["wd"].wait()
    pl.semaphore_wait(bar, expected + 4 * ((NZ - o) // NZ) + lax.rem(o, 2))

    s_piece = sem_ids(1)
    send(pieces.at[1 - c], piece_in, s_piece, (sib, o))

    fetches["lens"].wait()
    fetches["feat"].wait()
    length = lens[t]
    rim[0] = feat[0:24, :].astype(F32).astype(BF16)
    tail = feat[0:64, :].astype(F32)[40:64]
    for q in range(1, 4):
        tail = jnp.where(length == q + 1, feat[64 * q : 64 * q + 64, :].astype(F32)[40:64], tail)
    rim[1] = tail.astype(BF16)
    s_halo = sem_ids(2)
    send(rim.at[1], halo.at[0], s_halo, (up_t, o))
    send(rim.at[0], halo.at[1], s_halo + 1, (dn_t, o))

    arrived(piece_in, s_piece)
    mine = pieces[c].astype(F32)
    other = piece_in[...].astype(F32)
    t24[0:12, :] = jnp.where(c == 0, mine, other)
    t24[12:24, :] = jnp.where(c == 0, other, mine)
    wg[c, y, x] = t24[...].astype(BF16)

    near = (1, 7, 2, 6, 3, 5, 4)
    far = near[::-1]

    def row_of(k):
        return lax.rem(y + NY - k, NY)

    def share_x(buf, row, sem):
        for k in range(1, NX):
            send(buf.at[row, x], buf.at[row, x], sem + k - 1, (tile_at(y, lax.rem(x + k, NX)), o))

    def gather_start(buf, s_y, s_x):
        for k in far:
            send(buf.at[y, x], buf.at[y, x], s_y + k - 1, (tile_at(lax.rem(y + k, NY), x), o))
        share_x(buf, y, s_x)

    def gather_relay(buf, s_y, s_x, ks):
        for k in ks:
            row = row_of(k)
            arrived(buf.at[row, x], s_y + k - 1)
            share_x(buf, row, s_x + 3 * k)

    def gather_row(buf, s_x, k):
        row = row_of(k)
        for n in range(1, NX):
            arrived(buf.at[row, lax.rem(x + NX - n, NX)], s_x + 3 * k + n - 1)
        return row

    s_wy = sem_ids(NY - 1)
    s_wx = sem_ids(3 * NY)
    s_ws = sem_ids(NY)
    wg_c = wg.at[c]
    wg_o = wg.at[1 - c]
    gather_start(wg_c, s_wy, s_wx)

    for name in ("tissue", "dk", "gain", "scale", "cot", "bias"):
        fetches[name].wait()
    gain = gain1[...].reshape(1, D)
    scale = scale1[...].reshape(1, D)
    frame[...] = jnp.zeros_like(frame)
    for q in range(4):
        rows = slice(64 * q, 64 * q + 64)
        live = length > q
        keep = jnp.where(live, tissue[q], 0).astype(F32)
        f = feat[rows, :].astype(F32)
        if q:
            f = jnp.where(live, f, 0.0)
        for ch in range(CH):
            frame[ch, 3 + 8 * q : 11 + 8 * q, 3:11, :] = f[:, 128 * ch : 128 * ch + 128].reshape(8, 8, 128)
        left[1, rows, :] = ((keep * scale) * cot[rows, :].astype(F32)).astype(BF16)

    arrived(halo.at[0], s_halo)
    arrived(halo.at[1], s_halo + 1)
    before = jnp.where(t > 0, halo[0].astype(F32), 0.0)
    after = jnp.where(t < NT - 1, halo[1].astype(F32), 0.0)
    for ch in range(CH):
        lanes = slice(128 * ch, 128 * ch + 128)
        frame[ch, 0:3, 3:11, :] = before[:, lanes].reshape(3, 8, 128)
        nxt = after[:, lanes].reshape(3, 8, 128)
        for q in range(1, 4):
            old = frame[ch, 3 + 8 * q : 6 + 8 * q, 3:11, :]
            frame[ch, 3 + 8 * q : 6 + 8 * q, 3:11, :] = jnp.where(length == q, nxt, old)
        frame[ch, 35:38, 3:11, :] = jnp.where(length == 4, nxt, 0.0)

    def conv_half(h):
        def chunk(ch, _):
            lanes = pl.ds(pl.multiple_of(ch * 128, 128), 128)
            acc = jnp.zeros((16, 8, 128), F32)
            for i in range(7):
                for j in range(7):
                    w = dk[i, j : j + 1, lanes].reshape(1, 1, 128)
                    acc = acc + w * frame[ch, 16 * h + i : 16 * h + i + 16, j : j + 8, :]
            mixed[128 * h : 128 * h + 128, lanes] = acc.reshape(128, 128)
            return 0

        lax.fori_loop(0, CH, chunk, 0)

    conv_half(0)
    gather_relay(wg_c, s_wy, s_wx, near[:4])
    conv_half(1)
    gather_relay(wg_c, s_wy, s_wx, near[4:6])

    for q in range(4):
        rows = slice(64 * q, 64 * q + 64)
        m = mixed[rows, :]
        shifted = m - jnp.sum(m, axis=-1, keepdims=True) * (1.0 / D)
        var = jnp.sum(shifted * shifted, axis=-1, keepdims=True) * (1.0 / D)
        inv = lax.rsqrt(var + 1e-06)
        centred = shifted * inv
        mixed[rows, :] = centred
        inv_s[rows, :] = inv
        left[0, rows, :] = (centred * gain).astype(BF16)

    gather_relay(wg_c, s_wy, s_wx, near[6:])

    def take(m, row):
        wm[m, row] = wg[m, row].astype(F32).reshape(96, HID).astype(BF16)

    for k in (0,) + near:
        row = gather_row(wg_c, s_wx, k)
        send(wg_c.at[row], wg_c.at[row], s_ws + k, (sib, o))
        take(c, row)
    for k in (0,) + near:
        row = row_of(k)
        arrived(wg_o.at[row], s_ws + k)
        take(1 - c, row)

    up_w = wm[0].reshape(D, HID)
    down_w = wm[1].reshape(D, HID)
    hidden = bdot(left[0], up_w) + bias1[...].reshape(1, HID)
    phi = 0.5 * (1.0 + lax.erf(hidden * INV_ROOT_TWO))
    right[1] = (hidden * phi).astype(BF16)
    grad_act = bdot(left[1], down_w)
    slope = phi + hidden * jnp.exp(-0.5 * hidden * hidden) * INV_ROOT_TAU
    right[0] = (grad_act * slope).astype(BF16)

    s_g = sem_ids(1)
    gs[...] = bdot(left[1 - c], right[1 - c], TN_DIMS).reshape(NY, NX, RB, HID).astype(BF16)
    send(gs, grv, s_g, (sib, o))

    def scatter_z(value, buf, slots, s0):
        buf[...] = value.reshape(NZ, OWN_TOK, D).astype(BF16)
        for k in far:
            dest = lax.rem(o + k, NZ)
            send(buf.at[dest], slots.at[k - 1], s0 + k - 1, (t, dest))

    def scatter_z_sum(buf, slots, s0):
        total = buf[o].astype(F32)
        for k in range(1, NZ):
            arrived(slots.at[k - 1], s0 + k - 1)
            total = total + slots[k - 1].astype(F32)
        return total

    s_z = sem_ids(NZ - 1)
    s_b = sem_ids(NZ - 1)
    gf[...] = bdot(left[c], right[c], TN_DIMS).reshape(NY, NX, RB, HID)
    scatter_z(bdot(right[0], up_w, NT_DIMS), zs, zr, s_z)

    s_rx = sem_ids(3 * NY)
    s_ry = sem_ids(NY - 1)
    arrived(grv, s_g)
    for k in far + (0,):
        row = lax.rem(y + k, NY)
        pair = gf[row] + grv[row].astype(F32)
        gf[row] = pair
        gb[row] = pair.astype(BF16)
        for n in range(1, NX):
            col = lax.rem(x + n, NX)
            send(gb.at[row, col], rx.at[row, n - 1], s_rx + 3 * k + n - 1, (tile_at(y, col), o))
    scatter_z(bdot(right[1], down_w, NT_DIMS), bs, br, s_b)
    total = None
    for k in far + (0,):
        row = lax.rem(y + k, NY)
        total = gf[row, x]
        for n in range(1, NX):
            arrived(rx.at[row, n - 1], s_rx + 3 * k + n - 1)
            total = total + rx[row, n - 1].astype(F32)
        if k:
            ty[row] = total.astype(BF16)
            send(ty.at[row], ry.at[k - 1], s_ry + k - 1, (tile_at(row, x), o))
    for k in near:
        arrived(ry.at[k - 1], s_ry + k - 1)
        total = total + ry[k - 1].astype(F32)
    grow[...] = total
    ga[y, x] = total.astype(BF16)
    s_gy = sem_ids(NY - 1)
    s_gx = sem_ids(3 * NY)
    gather_start(ga, s_gy, s_gx)

    grad_normed = scatter_z_sum(zs, zr, s_z)
    own_rows = pl.ds(pl.multiple_of(o * OWN_TOK, OWN_TOK), OWN_TOK)
    own_live = length > o // 2
    centred = mixed[own_rows, :]
    g = grad_normed * gain
    mean1 = jnp.sum(g, axis=-1, keepdims=True) * (1.0 / D)
    mean2 = jnp.sum(g * centred, axis=-1, keepdims=True) * (1.0 / D)
    grad_mixed = inv_s[own_rows, :] * (g - mean1 - centred * mean2)
    grad_mixed = jnp.where(own_live, grad_mixed, 0.0)
    hg[...] = grad_mixed.astype(BF16)
    s_h = sem_ids(2)
    s_ct = sem_ids(4)
    s_ch = sem_ids(1)
    send(hg, nb.at[0], s_h, (t, lax.rem(o + 1, NZ)))
    send(hg, nb.at[1], s_h + 1, (t, lax.rem(o + NZ - 1, NZ)))
    s_c4 = sem_ids(4)

    @pl.when(first_own)
    def _():
        for q in range(4):
            pltpu.make_async_remote_copy(
                src_ref=hg, dst_ref=chd, send_sem=ss.at[s_c4 + q], recv_sem=rs.at[s_ch],
                device_id=(dn_t, 2 * q + 1), device_id_type=MESH,
            ).start()

    @pl.when(odd_own)
    def _():
        q = o // 2
        pltpu.make_async_remote_copy(
            src_ref=hg, dst_ref=ct.at[q], send_sem=ss.at[s_c4], recv_sem=rs.at[s_ct + q],
            device_id=(up_t, 0), device_id_type=MESH,
        ).start()

    frame2[...] = jnp.zeros_like(frame2)
    for ch in range(CH):
        frame2[ch, 3:7, 3:11, :] = grad_mixed[:, 128 * ch : 128 * ch + 128].reshape(4, 8, 128)

    gather_relay(ga, s_gy, s_gx, near[:4])

    def put_before(block):
        rows3 = block.astype(F32)[8:32]
        for ch in range(CH):
            frame2[ch, 0:3, 3:11, :] = rows3[:, 128 * ch : 128 * ch + 128].reshape(3, 8, 128)

    def put_after(block):
        rows3 = block.astype(F32)[0:24]
        for ch in range(CH):
            frame2[ch, 7:10, 3:11, :] = rows3[:, 128 * ch : 128 * ch + 128].reshape(3, 8, 128)

    gather_relay(ga, s_gy, s_gx, near[4:])
    arrived(nb.at[0], s_h)
    arrived(nb.at[1], s_h + 1)

    @pl.when(first_own)
    def _():
        for q in range(4):
            arrived(ct.at[q], s_ct + q)
        prev_len = lens[dn_t]
        block = ct[0].astype(F32)
        for q in range(1, 4):
            block = jnp.where(prev_len == q + 1, ct[q].astype(F32), block)
        put_before(jnp.where(t > 0, block, 0.0))
        for q in range(4):
            pltpu.make_async_remote_copy(
                src_ref=hg, dst_ref=chd, send_sem=ss.at[s_c4 + q], recv_sem=rs.at[s_ch],
                device_id=(dn_t, 2 * q + 1), device_id_type=MESH,
            ).wait_send()

    @pl.when(jnp.logical_not(first_own))
    def _():
        put_before(nb[0])

    @pl.when(odd_own)
    def _():
        arrived(chd, s_ch)
        q = o // 2
        edge = jnp.where(t < NT - 1, chd[...].astype(F32), 0.0)
        put_after(jnp.where(length == q + 1, edge, nb[1].astype(F32)))
        pltpu.make_async_remote_copy(
            src_ref=hg, dst_ref=ct.at[q], send_sem=ss.at[s_c4], recv_sem=rs.at[s_ct + q],
            device_id=(up_t, 0), device_id_type=MESH,
        ).wait_send()

    @pl.when(jnp.logical_not(odd_own))
    def _():
        put_after(nb[1])

    def chunk2(ch, _):
        lanes = pl.ds(pl.multiple_of(ch * 128, 128), 128)
        acc = jnp.zeros((4, 8, 128), F32)
        for i in range(7):
            for j in range(7):
                w = dk[6 - i, 6 - j : 7 - j, lanes].reshape(1, 1, 128)
                acc = acc + w * frame2[ch, i : i + 4, j : j + 8, :]
        res = cot[own_rows, lanes].astype(F32) + acc.reshape(OWN_TOK, 128)
        gout_ref[:, lanes] = jnp.where(own_live, res, 0.0).astype(BF16)
        return 0

    lax.fori_loop(0, CH, chunk2, 0)

    branch = scatter_z_sum(bs, br, s_b)
    own_keep = jnp.where(own_live, tissue[o // 2], 0).astype(F32)
    res = feat[own_rows, :].astype(F32) + (own_keep * scale) * branch
    out_ref[...] = jnp.where(own_live, res, 0.0).astype(BF16)

    def gram_of(ks):
        for n, k in enumerate(ks):
            row = gather_row(ga, s_gx, k)
            gm16[n] = ga[row].astype(F32).reshape(96, HID).astype(BF16)
        g16 = gm16[0 : len(ks)].reshape(96 * len(ks), HID)
        return bdot(g16, g16, TN_DIMS)

    gram = gram_of((0,) + near[:4]) + gram_of(near[4:])
    eye = (
        lax.broadcasted_iota(jnp.int32, (HID, HID), 0) == lax.broadcasted_iota(jnp.int32, (HID, HID), 1)
    ).astype(F32)

    norm2 = jnp.sum(jnp.sum(gram * eye, axis=0, keepdims=True), axis=1, keepdims=True)
    root = lax.rsqrt(norm2 + EPS_NORM)
    gram = gram * (root * root)

    def poly(a):
        return NS_A * eye + NS_B * a + NS_C * f32dot(a, a)

    p0 = poly(gram)
    gram1 = f32dot(f32dot(gram, p0), p0)
    p1 = poly(gram1)
    xo[c] = f32dot(f32dot(grow[...] * root, p0), p1)
    s_x = sem_ids(1)
    send(xo.at[c], xo.at[c], s_x, (sib, o))
    arrived(xo.at[1 - c], s_x)
    mu_ref[...] = jnp.where(c == 0, xo[0, 0:12, :], xo[0, 12:24, :])
    md_ref[...] = jnp.where(c == 0, xo[1, 0:12, :], xo[1, 12:24, :])

    for cp in sent:
        cp.wait_send()


SEMS = 160


def shards(features, cotangent, depth_kernel, ln_gain, weight_up, bias_up, weight_down, layer_scale, tissue, lengths):
    vmem = pl.BlockSpec(memory_space=pltpu.VMEM)
    hbm = pl.BlockSpec(memory_space=pltpu.HBM)
    block4 = (NY, NX, RB, HID)
    scratch = [
        pltpu.SMEM((NT,), jnp.int32),
        pltpu.SMEM((4,), jnp.int32),
        pltpu.VMEM((TOK, D), BF16),
        pltpu.VMEM((TOK, D), BF16),
        pltpu.VMEM((7, 7, D), F32),
        pltpu.VMEM((D,), F32),
        pltpu.VMEM((HID,), F32),
        pltpu.VMEM((D,), F32),
        pltpu.VMEM((2, 12, HID), BF16),
        pltpu.VMEM((12, HID), BF16),
        pltpu.VMEM((24, HID), F32),
        pltpu.VMEM((2,) + block4, BF16),
        pltpu.VMEM((2, NY, 96, HID), BF16),
        pltpu.VMEM((2, 24, D), BF16),
        pltpu.VMEM((2, 24, D), BF16),
        pltpu.VMEM((CH, 38, 16, 128), F32),
        pltpu.VMEM((TOK, D), F32),
        pltpu.VMEM((TOK, 1), F32),
        pltpu.VMEM((2, TOK, D), BF16),
        pltpu.VMEM((2, TOK, HID), BF16),
        pltpu.VMEM((NZ, OWN_TOK, D), BF16),
        pltpu.VMEM((NZ - 1, OWN_TOK, D), BF16),
        pltpu.VMEM((NZ, OWN_TOK, D), BF16),
        pltpu.VMEM((NZ - 1, OWN_TOK, D), BF16),
        pltpu.VMEM(block4, BF16),
        pltpu.VMEM(block4, BF16),
        pltpu.VMEM(block4, F32),
        pltpu.VMEM(block4, BF16),
        pltpu.VMEM((NY, NX - 1, RB, HID), BF16),
        pltpu.VMEM((NY, RB, HID), BF16),
        pltpu.VMEM((NY - 1, RB, HID), BF16),
        pltpu.VMEM((RB, HID), F32),
        pltpu.VMEM(block4, BF16),
        pltpu.VMEM((NY, 96, HID), BF16),
        pltpu.VMEM((OWN_TOK, D), BF16),
        pltpu.VMEM((2, OWN_TOK, D), BF16),
        pltpu.VMEM((4, OWN_TOK, D), BF16),
        pltpu.VMEM((OWN_TOK, D), BF16),
        pltpu.VMEM((CH, 10, 16, 128), F32),
        pltpu.VMEM((2, RB, HID), F32),
        pltpu.SemaphoreType.DMA((SEMS,)),
        pltpu.SemaphoreType.DMA((SEMS,)),
        pltpu.SemaphoreType.DMA((10,)),
    ]
    outs = pl.pallas_call(
        body,
        out_shape=(
            jax.ShapeDtypeStruct((OWN_TOK, D), BF16),
            jax.ShapeDtypeStruct((OWN_TOK, D), BF16),
            jax.ShapeDtypeStruct((12, HID), F32),
            jax.ShapeDtypeStruct((12, HID), F32),
        ),
        in_specs=[hbm] * 10,
        out_specs=(vmem,) * 4,
        scratch_shapes=scratch,
        compiler_params=pltpu.CompilerParams(
            collective_id=0, has_side_effects=True, vmem_limit_bytes=48 << 20
        ),
    )(
        lengths,
        tissue.reshape(4),
        features.reshape(TOK, D),
        cotangent.reshape(TOK, D),
        depth_kernel,
        ln_gain,
        weight_up,
        bias_up,
        weight_down.T,
        layer_scale,
    )
    block_out, grad_features, muon_up, muon_down_t = outs
    return (
        block_out.reshape(4, 8, D),
        grad_features.reshape(4, 8, D),
        muon_up,
        muon_down_t.T,
    )


def solution(mesh):
    in_specs = (
        P("tile", None, None),
        P("tile", None, None),
        P(),
        P(),
        P("tile", "own"),
        P("own"),
        P("own", "tile"),
        P(),
        P("tile", None),
        P(),
    )
    out_specs = (
        P(("tile", "own"), None, None),
        P(("tile", "own"), None, None),
        P("tile", "own"),
        P("own", "tile"),
    )
    return jax.shard_map(shards, mesh=mesh, in_specs=in_specs, out_specs=out_specs, check_vma=False)
```

```python
import jax
import jax.numpy as jnp
from jax import lax
from jax.experimental import pallas as pl
from jax.experimental.pallas import tpu as pltpu
from jax.sharding import PartitionSpec as P

MESH = pl.DeviceIdType.MESH
F32 = jnp.float32
BF16 = jnp.bfloat16

NY, NX, NZ = 8, 4, 8
NT = NY * NX * 2
D = 768
HID = 384
TOK = 256
CH = D // 128
RB = 24
OWN_TOK = 32

INV_ROOT_TWO = 0.7071067811865476
INV_ROOT_TAU = 0.3989422804014327
NS_A = 3.4445
NS_B = -4.775
NS_C = 2.0315
EPS_NORM = 1e-06
HIGH = lax.Precision.HIGH


def f32dot(a, b, dims=(((1,), (0,)), ((), ()))):
    return lax.dot_general(a, b, dims, precision=HIGH, preferred_element_type=F32)


def bdot(a, b, dims=(((1,), (0,)), ((), ()))):
    return lax.dot_general(a, b, dims, preferred_element_type=F32)


NT_DIMS = (((1,), (1,)), ((), ()))
TN_DIMS = (((0,), (0,)), ((), ()))


def body(
    lens_h, tissue_h, feat_h, cot_h, dk_h, gain_h, wu_h, bias_h, wd_h, scale_h,
    out_ref, gout_ref, mu_ref, md_ref,
    lens, tissue, feat, cot, dk, gain1, bias1, scale1, pieces, piece_in, t24, wg, wm, rim, halo, frame, mixed, inv_s, left, right,
    zs, zr, bs, br, gs, grv, gf, gb, rx, ty, ry, grow, ga, gm16, hg, nb, ct, chd, frame2, xo,
    ss, rs, ls,
):
    t = lax.axis_index("tile")
    o = lax.axis_index("own")
    c = lax.rem(t, 2)
    chip = t // 2
    x = lax.rem(chip, NX)
    y = chip // NX
    sib = t + 1 - 2 * c

    def tile_at(yy, xx):
        return (yy * NX + xx) * 2 + c

    counter = [0]
    sent = []

    def sem_ids(n):
        first = counter[0]
        counter[0] += n
        return first

    def copy(src, dst, sem, dev):
        return pltpu.make_async_remote_copy(
            src_ref=src, dst_ref=dst, send_sem=ss.at[sem], recv_sem=rs.at[sem],
            device_id=dev, device_id_type=MESH,
        )

    def send(src, dst, sem, dev):
        cp = copy(src, dst, sem, dev)
        cp.start()
        sent.append(cp)

    def arrived(dst, sem):
        copy(dst, dst, sem, (t, o)).wait_recv()

    fetches = {}
    for n, (name, src, dst) in enumerate(
        (
            ("wu", wu_h, pieces.at[0]), ("wd", wd_h, pieces.at[1]), ("lens", lens_h, lens),
            ("feat", feat_h, feat), ("tissue", tissue_h, tissue), ("dk", dk_h, dk), ("gain", gain_h, gain1),
            ("scale", scale_h, scale1), ("cot", cot_h, cot), ("bias", bias_h, bias1),
        )
    ):
        fetches[name] = pltpu.make_async_copy(src, dst, ls.at[n])
        fetches[name].start()

    bar = pltpu.get_barrier_semaphore()

    def greet(dev):
        pl.semaphore_signal(bar, inc=1, device_id=dev, device_id_type=MESH)

    up_t = lax.rem(t + 1, NT)
    dn_t = lax.rem(t + NT - 1, NT)
    greet((sib, o))
    for k in range(1, NY):
        greet((tile_at(lax.rem(y + k, NY), x), o))
    for k in range(1, NX):
        greet((tile_at(y, lax.rem(x + k, NX)), o))
    for k in range(1, NZ):
        greet((t, lax.rem(o + k, NZ)))
    greet((up_t, o))
    greet((dn_t, o))
    first_own = o == 0
    odd_own = lax.rem(o, 2) == 1

    @pl.when(first_own)
    def _():
        for q in range(4):
            greet((dn_t, 2 * q + 1))

    @pl.when(odd_own)
    def _():
        greet((up_t, 0))

    expected = 1 + (NY - 1) + (NX - 1) + (NZ - 1) + 2
    fetches["wu"].wait()
    fetches["wd"].wait()
    pl.semaphore_wait(bar, expected + 4 * ((NZ - o) // NZ) + lax.rem(o, 2))

    s_piece = sem_ids(1)
    send(pieces.at[1 - c], piece_in, s_piece, (sib, o))

    fetches["lens"].wait()
    fetches["feat"].wait()
    length = lens[t]
    rim[0] = feat[0:24, :].astype(F32).astype(BF16)
    tail = feat[0:64, :].astype(F32)[40:64]
    for q in range(1, 4):
        tail = jnp.where(length == q + 1, feat[64 * q : 64 * q + 64, :].astype(F32)[40:64], tail)
    rim[1] = tail.astype(BF16)
    s_halo = sem_ids(2)
    send(rim.at[1], halo.at[0], s_halo, (up_t, o))
    send(rim.at[0], halo.at[1], s_halo + 1, (dn_t, o))

    arrived(piece_in, s_piece)
    mine = pieces[c].astype(F32)
    other = piece_in[...].astype(F32)
    t24[0:12, :] = jnp.where(c == 0, mine, other)
    t24[12:24, :] = jnp.where(c == 0, other, mine)
    wg[c, y, x] = t24[...].astype(BF16)

    near = (1, 7, 2, 6, 3, 5, 4)
    far = near[::-1]

    def row_of(k):
        return lax.rem(y + NY - k, NY)

    def share_x(buf, row, sem):
        for k in range(1, NX):
            send(buf.at[row, x], buf.at[row, x], sem + k - 1, (tile_at(y, lax.rem(x + k, NX)), o))

    def gather_start(buf, s_y, s_x):
        for k in far:
            send(buf.at[y, x], buf.at[y, x], s_y + k - 1, (tile_at(lax.rem(y + k, NY), x), o))
        share_x(buf, y, s_x)

    def gather_relay(buf, s_y, s_x, ks):
        for k in ks:
            row = row_of(k)
            arrived(buf.at[row, x], s_y + k - 1)
            share_x(buf, row, s_x + 3 * k)

    def gather_row(buf, s_x, k):
        row = row_of(k)
        for n in range(1, NX):
            arrived(buf.at[row, lax.rem(x + NX - n, NX)], s_x + 3 * k + n - 1)
        return row

    s_wy = sem_ids(NY - 1)
    s_wx = sem_ids(3 * NY)
    s_ws = sem_ids(NY)
    wg_c = wg.at[c]
    wg_o = wg.at[1 - c]
    gather_start(wg_c, s_wy, s_wx)

    for name in ("tissue", "dk", "gain", "scale", "cot", "bias"):
        fetches[name].wait()
    gain = gain1[...].reshape(1, D)
    scale = scale1[...].reshape(1, D)
    frame[...] = jnp.zeros_like(frame)
    for q in range(4):
        rows = slice(64 * q, 64 * q + 64)
        live = length > q
        keep = jnp.where(live, tissue[q], 0).astype(F32)
        f = feat[rows, :].astype(F32)
        if q:
            f = jnp.where(live, f, 0.0)
        for ch in range(CH):
            frame[ch, 3 + 8 * q : 11 + 8 * q, 3:11, :] = f[:, 128 * ch : 128 * ch + 128].reshape(8, 8, 128)
        left[1, rows, :] = ((keep * scale) * cot[rows, :].astype(F32)).astype(BF16)

    arrived(halo.at[0], s_halo)
    arrived(halo.at[1], s_halo + 1)
    before = jnp.where(t > 0, halo[0].astype(F32), 0.0)
    after = jnp.where(t < NT - 1, halo[1].astype(F32), 0.0)
    for ch in range(CH):
        lanes = slice(128 * ch, 128 * ch + 128)
        frame[ch, 0:3, 3:11, :] = before[:, lanes].reshape(3, 8, 128)
        nxt = after[:, lanes].reshape(3, 8, 128)
        for q in range(1, 4):
            old = frame[ch, 3 + 8 * q : 6 + 8 * q, 3:11, :]
            frame[ch, 3 + 8 * q : 6 + 8 * q, 3:11, :] = jnp.where(length == q, nxt, old)
        frame[ch, 35:38, 3:11, :] = jnp.where(length == 4, nxt, 0.0)

    def conv_half(h):
        def chunk(ch, _):
            lanes = pl.ds(pl.multiple_of(ch * 128, 128), 128)
            acc = jnp.zeros((16, 8, 128), F32)
            for i in range(7):
                for j in range(7):
                    w = dk[i, j : j + 1, lanes].reshape(1, 1, 128)
                    acc = acc + w * frame[ch, 16 * h + i : 16 * h + i + 16, j : j + 8, :]
            mixed[128 * h : 128 * h + 128, lanes] = acc.reshape(128, 128)
            return 0

        lax.fori_loop(0, CH, chunk, 0)

    conv_half(0)
    gather_relay(wg_c, s_wy, s_wx, near[:4])
    conv_half(1)
    gather_relay(wg_c, s_wy, s_wx, near[4:6])

    for q in range(4):
        rows = slice(64 * q, 64 * q + 64)
        m = mixed[rows, :]
        shifted = m - jnp.sum(m, axis=-1, keepdims=True) * (1.0 / D)
        var = jnp.sum(shifted * shifted, axis=-1, keepdims=True) * (1.0 / D)
        inv = lax.rsqrt(var + 1e-06)
        centred = shifted * inv
        mixed[rows, :] = centred
        inv_s[rows, :] = inv
        left[0, rows, :] = (centred * gain).astype(BF16)

    gather_relay(wg_c, s_wy, s_wx, near[6:])

    def take(m, row):
        wm[m, row] = wg[m, row].astype(F32).reshape(96, HID).astype(BF16)

    for k in (0,) + near:
        row = gather_row(wg_c, s_wx, k)
        send(wg_c.at[row], wg_c.at[row], s_ws + k, (sib, o))
        take(c, row)
    for k in (0,) + near:
        row = row_of(k)
        arrived(wg_o.at[row], s_ws + k)
        take(1 - c, row)

    up_w = wm[0].reshape(D, HID)
    down_w = wm[1].reshape(D, HID)
    hidden = bdot(left[0], up_w) + bias1[...].reshape(1, HID)
    phi = 0.5 * (1.0 + lax.erf(hidden * INV_ROOT_TWO))
    right[1] = (hidden * phi).astype(BF16)
    grad_act = bdot(left[1], down_w)
    slope = phi + hidden * jnp.exp(-0.5 * hidden * hidden) * INV_ROOT_TAU
    right[0] = (grad_act * slope).astype(BF16)

    s_g = sem_ids(1)
    gs[...] = bdot(left[1 - c], right[1 - c], TN_DIMS).reshape(NY, NX, RB, HID).astype(BF16)
    send(gs, grv, s_g, (sib, o))

    def scatter_z(value, buf, slots, s0):
        buf[...] = value.reshape(NZ, OWN_TOK, D).astype(BF16)
        for k in far:
            dest = lax.rem(o + k, NZ)
            send(buf.at[dest], slots.at[k - 1], s0 + k - 1, (t, dest))

    def scatter_z_sum(buf, slots, s0):
        total = buf[o].astype(F32)
        for k in range(1, NZ):
            arrived(slots.at[k - 1], s0 + k - 1)
            total = total + slots[k - 1].astype(F32)
        return total

    s_z = sem_ids(NZ - 1)
    s_b = sem_ids(NZ - 1)
    gf[...] = bdot(left[c], right[c], TN_DIMS).reshape(NY, NX, RB, HID)
    scatter_z(bdot(right[0], up_w, NT_DIMS), zs, zr, s_z)

    s_rx = sem_ids(3 * NY)
    s_ry = sem_ids(NY - 1)
    arrived(grv, s_g)
    for k in far + (0,):
        row = lax.rem(y + k, NY)
        pair = gf[row] + grv[row].astype(F32)
        gf[row] = pair
        gb[row] = pair.astype(BF16)
        for n in range(1, NX):
            col = lax.rem(x + n, NX)
            send(gb.at[row, col], rx.at[row, n - 1], s_rx + 3 * k + n - 1, (tile_at(y, col), o))
    scatter_z(bdot(right[1], down_w, NT_DIMS), bs, br, s_b)
    total = None
    for k in far + (0,):
        row = lax.rem(y + k, NY)
        total = gf[row, x]
        for n in range(1, NX):
            arrived(rx.at[row, n - 1], s_rx + 3 * k + n - 1)
            total = total + rx[row, n - 1].astype(F32)
        if k:
            ty[row] = total.astype(BF16)
            send(ty.at[row], ry.at[k - 1], s_ry + k - 1, (tile_at(row, x), o))
    for k in near:
        arrived(ry.at[k - 1], s_ry + k - 1)
        total = total + ry[k - 1].astype(F32)
    grow[...] = total
    ga[y, x] = total.astype(BF16)
    s_gy = sem_ids(NY - 1)
    s_gx = sem_ids(3 * NY)
    gather_start(ga, s_gy, s_gx)

    grad_normed = scatter_z_sum(zs, zr, s_z)
    own_rows = pl.ds(pl.multiple_of(o * OWN_TOK, OWN_TOK), OWN_TOK)
    own_live = length > o // 2
    centred = mixed[own_rows, :]
    g = grad_normed * gain
    mean1 = jnp.sum(g, axis=-1, keepdims=True) * (1.0 / D)
    mean2 = jnp.sum(g * centred, axis=-1, keepdims=True) * (1.0 / D)
    grad_mixed = inv_s[own_rows, :] * (g - mean1 - centred * mean2)
    grad_mixed = jnp.where(own_live, grad_mixed, 0.0)
    hg[...] = grad_mixed.astype(BF16)
    s_h = sem_ids(2)
    s_ct = sem_ids(4)
    s_ch = sem_ids(1)
    send(hg, nb.at[0], s_h, (t, lax.rem(o + 1, NZ)))
    send(hg, nb.at[1], s_h + 1, (t, lax.rem(o + NZ - 1, NZ)))
    s_c4 = sem_ids(4)

    @pl.when(first_own)
    def _():
        for q in range(4):
            pltpu.make_async_remote_copy(
                src_ref=hg, dst_ref=chd, send_sem=ss.at[s_c4 + q], recv_sem=rs.at[s_ch],
                device_id=(dn_t, 2 * q + 1), device_id_type=MESH,
            ).start()

    @pl.when(odd_own)
    def _():
        q = o // 2
        pltpu.make_async_remote_copy(
            src_ref=hg, dst_ref=ct.at[q], send_sem=ss.at[s_c4], recv_sem=rs.at[s_ct + q],
            device_id=(up_t, 0), device_id_type=MESH,
        ).start()

    frame2[...] = jnp.zeros_like(frame2)
    for ch in range(CH):
        frame2[ch, 3:7, 3:11, :] = grad_mixed[:, 128 * ch : 128 * ch + 128].reshape(4, 8, 128)

    gather_relay(ga, s_gy, s_gx, near[:4])

    def put_before(block):
        rows3 = block.astype(F32)[8:32]
        for ch in range(CH):
            frame2[ch, 0:3, 3:11, :] = rows3[:, 128 * ch : 128 * ch + 128].reshape(3, 8, 128)

    def put_after(block):
        rows3 = block.astype(F32)[0:24]
        for ch in range(CH):
            frame2[ch, 7:10, 3:11, :] = rows3[:, 128 * ch : 128 * ch + 128].reshape(3, 8, 128)

    gather_relay(ga, s_gy, s_gx, near[4:])
    arrived(nb.at[0], s_h)
    arrived(nb.at[1], s_h + 1)

    @pl.when(first_own)
    def _():
        for q in range(4):
            arrived(ct.at[q], s_ct + q)
        prev_len = lens[dn_t]
        block = ct[0].astype(F32)
        for q in range(1, 4):
            block = jnp.where(prev_len == q + 1, ct[q].astype(F32), block)
        put_before(jnp.where(t > 0, block, 0.0))
        for q in range(4):
            pltpu.make_async_remote_copy(
                src_ref=hg, dst_ref=chd, send_sem=ss.at[s_c4 + q], recv_sem=rs.at[s_ch],
                device_id=(dn_t, 2 * q + 1), device_id_type=MESH,
            ).wait_send()

    @pl.when(jnp.logical_not(first_own))
    def _():
        put_before(nb[0])

    @pl.when(odd_own)
    def _():
        arrived(chd, s_ch)
        q = o // 2
        edge = jnp.where(t < NT - 1, chd[...].astype(F32), 0.0)
        put_after(jnp.where(length == q + 1, edge, nb[1].astype(F32)))
        pltpu.make_async_remote_copy(
            src_ref=hg, dst_ref=ct.at[q], send_sem=ss.at[s_c4], recv_sem=rs.at[s_ct + q],
            device_id=(up_t, 0), device_id_type=MESH,
        ).wait_send()

    @pl.when(jnp.logical_not(odd_own))
    def _():
        put_after(nb[1])

    def chunk2(ch, _):
        lanes = pl.ds(pl.multiple_of(ch * 128, 128), 128)
        acc = jnp.zeros((4, 8, 128), F32)
        for i in range(7):
            for j in range(7):
                w = dk[6 - i, 6 - j : 7 - j, lanes].reshape(1, 1, 128)
                acc = acc + w * frame2[ch, i : i + 4, j : j + 8, :]
        res = cot[own_rows, lanes].astype(F32) + acc.reshape(OWN_TOK, 128)
        gout_ref[:, lanes] = jnp.where(own_live, res, 0.0).astype(BF16)
        return 0

    lax.fori_loop(0, CH, chunk2, 0)

    branch = scatter_z_sum(bs, br, s_b)
    own_keep = jnp.where(own_live, tissue[o // 2], 0).astype(F32)
    res = feat[own_rows, :].astype(F32) + (own_keep * scale) * branch
    out_ref[...] = jnp.where(own_live, res, 0.0).astype(BF16)

    def gram_of(ks):
        for n, k in enumerate(ks):
            row = gather_row(ga, s_gx, k)
            gm16[n] = ga[row].astype(F32).reshape(96, HID).astype(BF16)
        g16 = gm16[0 : len(ks)].reshape(96 * len(ks), HID)
        return bdot(g16, g16, TN_DIMS)

    gram = gram_of((0,) + near[:4]) + gram_of(near[4:])
    eye = (
        lax.broadcasted_iota(jnp.int32, (HID, HID), 0) == lax.broadcasted_iota(jnp.int32, (HID, HID), 1)
    ).astype(F32)

    norm2 = jnp.sum(jnp.sum(gram * eye, axis=0, keepdims=True), axis=1, keepdims=True)
    root = lax.rsqrt(norm2 + EPS_NORM)
    gram = gram * (root * root)

    def poly(a):
        return NS_A * eye + NS_B * a + NS_C * f32dot(a, a)

    p0 = poly(gram)
    gram1 = f32dot(f32dot(gram, p0), p0)
    p1 = poly(gram1)
    xo[c] = f32dot(f32dot(grow[...] * root, p0), p1)
    s_x = sem_ids(1)
    send(xo.at[c], xo.at[c], s_x, (sib, o))
    arrived(xo.at[1 - c], s_x)
    mu_ref[...] = jnp.where(c == 0, xo[0, 0:12, :], xo[0, 12:24, :])
    md_ref[...] = jnp.where(c == 0, xo[1, 0:12, :], xo[1, 12:24, :])

    for cp in sent:
        cp.wait_send()


SEMS = 160


def shards(features, cotangent, depth_kernel, ln_gain, weight_up, bias_up, weight_down, layer_scale, tissue, lengths):
    vmem = pl.BlockSpec(memory_space=pltpu.VMEM)
    hbm = pl.BlockSpec(memory_space=pltpu.HBM)
    block4 = (NY, NX, RB, HID)
    scratch = [
        pltpu.SMEM((NT,), jnp.int32),
        pltpu.SMEM((4,), jnp.int32),
        pltpu.VMEM((TOK, D), BF16),
        pltpu.VMEM((TOK, D), BF16),
        pltpu.VMEM((7, 7, D), F32),
        pltpu.VMEM((D,), F32),
        pltpu.VMEM((HID,), F32),
        pltpu.VMEM((D,), F32),
        pltpu.VMEM((2, 12, HID), BF16),
        pltpu.VMEM((12, HID), BF16),
        pltpu.VMEM((24, HID), F32),
        pltpu.VMEM((2,) + block4, BF16),
        pltpu.VMEM((2, NY, 96, HID), BF16),
        pltpu.VMEM((2, 24, D), BF16),
        pltpu.VMEM((2, 24, D), BF16),
        pltpu.VMEM((CH, 38, 16, 128), F32),
        pltpu.VMEM((TOK, D), F32),
        pltpu.VMEM((TOK, 1), F32),
        pltpu.VMEM((2, TOK, D), BF16),
        pltpu.VMEM((2, TOK, HID), BF16),
        pltpu.VMEM((NZ, OWN_TOK, D), BF16),
        pltpu.VMEM((NZ - 1, OWN_TOK, D), BF16),
        pltpu.VMEM((NZ, OWN_TOK, D), BF16),
        pltpu.VMEM((NZ - 1, OWN_TOK, D), BF16),
        pltpu.VMEM(block4, BF16),
        pltpu.VMEM(block4, BF16),
        pltpu.VMEM(block4, F32),
        pltpu.VMEM(block4, BF16),
        pltpu.VMEM((NY, NX - 1, RB, HID), BF16),
        pltpu.VMEM((NY, RB, HID), BF16),
        pltpu.VMEM((NY - 1, RB, HID), BF16),
        pltpu.VMEM((RB, HID), F32),
        pltpu.VMEM(block4, BF16),
        pltpu.VMEM((NY, 96, HID), BF16),
        pltpu.VMEM((OWN_TOK, D), BF16),
        pltpu.VMEM((2, OWN_TOK, D), BF16),
        pltpu.VMEM((4, OWN_TOK, D), BF16),
        pltpu.VMEM((OWN_TOK, D), BF16),
        pltpu.VMEM((CH, 10, 16, 128), F32),
        pltpu.VMEM((2, RB, HID), F32),
        pltpu.SemaphoreType.DMA((SEMS,)),
        pltpu.SemaphoreType.DMA((SEMS,)),
        pltpu.SemaphoreType.DMA((10,)),
    ]
    outs = pl.pallas_call(
        body,
        out_shape=(
            jax.ShapeDtypeStruct((OWN_TOK, D), BF16),
            jax.ShapeDtypeStruct((OWN_TOK, D), BF16),
            jax.ShapeDtypeStruct((12, HID), F32),
            jax.ShapeDtypeStruct((12, HID), F32),
        ),
        in_specs=[hbm] * 10,
        out_specs=(vmem,) * 4,
        scratch_shapes=scratch,
        compiler_params=pltpu.CompilerParams(
            collective_id=0, has_side_effects=True, vmem_limit_bytes=62 << 20
        ),
    )(
        lengths,
        tissue.reshape(4),
        features.reshape(TOK, D),
        cotangent.reshape(TOK, D),
        depth_kernel,
        ln_gain,
        weight_up,
        bias_up,
        weight_down.T,
        layer_scale,
    )
    block_out, grad_features, muon_up, muon_down_t = outs
    return (
        block_out.reshape(4, 8, D),
        grad_features.reshape(4, 8, D),
        muon_up,
        muon_down_t.T,
    )


def solution(mesh):
    in_specs = (
        P("tile", None, None),
        P("tile", None, None),
        P(),
        P(),
        P("tile", "own"),
        P("own"),
        P("own", "tile"),
        P(),
        P("tile", None),
        P(),
    )
    out_specs = (
        P(("tile", "own"), None, None),
        P(("tile", "own"), None, None),
        P("tile", "own"),
        P("own", "tile"),
    )
    return jax.shard_map(shards, mesh=mesh, in_specs=in_specs, out_specs=out_specs, check_vma=False)
```

```python
import jax
import jax.numpy as jnp
from jax import lax
from jax.experimental import pallas as pl
from jax.experimental.pallas import tpu as pltpu
from jax.sharding import PartitionSpec as P

MESH = pl.DeviceIdType.MESH
F32 = jnp.float32
BF16 = jnp.bfloat16

NY, NX, NZ = 8, 4, 8
NT = NY * NX * 2
D = 768
HID = 384
TOK = 256
CH = D // 128
RB = 24
OWN_TOK = 32

INV_ROOT_TWO = 0.7071067811865476
INV_ROOT_TAU = 0.3989422804014327
NS_A = 3.4445
NS_B = -4.775
NS_C = 2.0315
EPS_NORM = 1e-06


def bdot(a, b, dims=(((1,), (0,)), ((), ()))):
    return lax.dot_general(a, b, dims, preferred_element_type=F32)


NT_DIMS = (((1,), (1,)), ((), ()))
TN_DIMS = (((0,), (0,)), ((), ()))


def body(
    lens_h, tissue_h, feat_h, cot_h, dk_h, gain_h, wu_h, bias_h, wd_h, scale_h,
    tok_ref, muon_ref,
    lens, tissue, feat, cot, dk, gain1, bias1, scale1, t96, wg, wm, rim, halo, frame, mixed, inv_s, left, right,
    zs, zr, bs, br, gs, grv, gf, gb, rx, ty, ry, grow, ga, gm16, hg, nb, ct, chd, frame2, xo,
    ss, rs, ls,
):
    t = lax.axis_index("tile")
    o = lax.axis_index("own")
    c = lax.rem(t, 2)
    chip = t // 2
    x = lax.rem(chip, NX)
    y = chip // NX
    sib = t + 1 - 2 * c

    def tile_at(yy, xx):
        return (yy * NX + xx) * 2 + c

    counter = [0]
    sent = []

    def sem_ids(n):
        first = counter[0]
        counter[0] += n
        return first

    def copy(src, dst, sem, dev):
        return pltpu.make_async_remote_copy(
            src_ref=src, dst_ref=dst, send_sem=ss.at[sem], recv_sem=rs.at[sem],
            device_id=dev, device_id_type=MESH,
        )

    def send(src, dst, sem, dev):
        cp = copy(src, dst, sem, dev)
        cp.start()
        sent.append(cp)

    def arrived(dst, sem):
        copy(dst, dst, sem, (t, o)).wait_recv()

    fetches = {}
    for n, (name, src, dst) in enumerate(
        (
            ("wu", wu_h, wg.at[0, y, x, c]), ("wd", wd_h, wg.at[1, y, x, c]), ("lens", lens_h, lens),
            ("feat", feat_h, feat), ("tissue", tissue_h, tissue), ("dk", dk_h, dk), ("gain", gain_h, gain1),
            ("scale", scale_h, scale1), ("cot", cot_h, cot), ("bias", bias_h, bias1),
        )
    ):
        fetches[name] = pltpu.make_async_copy(src, dst, ls.at[n])
        fetches[name].start()

    bar = pltpu.get_barrier_semaphore()

    def greet(dev):
        pl.semaphore_signal(bar, inc=1, device_id=dev, device_id_type=MESH)

    up_t = lax.rem(t + 1, NT)
    dn_t = lax.rem(t + NT - 1, NT)
    greet((sib, o))
    for k in range(1, NY):
        greet((tile_at(lax.rem(y + k, NY), x), o))
    for k in range(1, NX):
        greet((tile_at(y, lax.rem(x + k, NX)), o))
    for k in range(1, NZ):
        greet((t, lax.rem(o + k, NZ)))
    greet((up_t, o))
    greet((dn_t, o))
    first_own = o == 0
    odd_own = lax.rem(o, 2) == 1

    @pl.when(first_own)
    def _():
        for q in range(4):
            greet((dn_t, 2 * q + 1))

    @pl.when(odd_own)
    def _():
        greet((up_t, 0))

    expected = 1 + (NY - 1) + (NX - 1) + (NZ - 1) + 2
    fetches["wu"].wait()
    fetches["wd"].wait()
    pl.semaphore_wait(bar, expected + 4 * ((NZ - o) // NZ) + lax.rem(o, 2))

    near = (1, 7, 2, 6, 3, 5, 4)
    far = near[::-1]

    def row_of(k):
        return lax.rem(y + NY - k, NY)

    def share_x(at, row, sem):
        for k in range(1, NX):
            send(at(row, x), at(row, x), sem + k - 1, (tile_at(y, lax.rem(x + k, NX)), o))

    def gather_start(at, s_y, s_x):
        for k in far:
            send(at(y, x), at(y, x), s_y + k - 1, (tile_at(lax.rem(y + k, NY), x), o))
        share_x(at, y, s_x)

    def gather_relay(at, s_y, s_x, ks):
        for k in ks:
            row = row_of(k)
            arrived(at(row, x), s_y + k - 1)
            share_x(at, row, s_x + 3 * k)

    def gather_row(at, s_x, k):
        row = row_of(k)
        for n in range(1, NX):
            arrived(at(row, lax.rem(x + NX - n, NX)), s_x + 3 * k + n - 1)
        return row

    def weight_at(row, col):
        return wg.at[:, row, col, c]

    def grad_at(row, col):
        return ga.at[row, col]

    s_wy = sem_ids(NY - 1)
    s_wx = sem_ids(3 * NY)
    s_ws = sem_ids(NY)
    gather_start(weight_at, s_wy, s_wx)

    fetches["lens"].wait()
    fetches["feat"].wait()
    length = lens[t]
    rim[0] = feat[0:24, :].astype(F32).astype(BF16)
    tail = feat[0:64, :].astype(F32)[40:64]
    for q in range(1, 4):
        tail = jnp.where(length == q + 1, feat[64 * q : 64 * q + 64, :].astype(F32)[40:64], tail)
    rim[1] = tail.astype(BF16)
    s_halo = sem_ids(2)
    send(rim.at[1], halo.at[0], s_halo, (up_t, o))
    send(rim.at[0], halo.at[1], s_halo + 1, (dn_t, o))

    for name in ("tissue", "dk", "gain", "scale", "cot", "bias"):
        fetches[name].wait()
    gain = gain1[...].reshape(1, D)
    scale = scale1[...].reshape(1, D)
    frame[...] = jnp.zeros_like(frame)
    for q in range(4):
        rows = slice(64 * q, 64 * q + 64)
        live = length > q
        keep = jnp.where(live, tissue[q], 0).astype(F32)
        f = feat[rows, :].astype(F32)
        if q:
            f = jnp.where(live, f, 0.0)
        for ch in range(CH):
            frame[ch, 3 + 8 * q : 11 + 8 * q, 3:11, :] = f[:, 128 * ch : 128 * ch + 128].reshape(8, 8, 128)
        left[1, rows, :] = ((keep * scale) * cot[rows, :].astype(F32)).astype(BF16)

    arrived(halo.at[0], s_halo)
    arrived(halo.at[1], s_halo + 1)
    before = jnp.where(t > 0, halo[0].astype(F32), 0.0)
    after = jnp.where(t < NT - 1, halo[1].astype(F32), 0.0)
    for ch in range(CH):
        lanes = slice(128 * ch, 128 * ch + 128)
        frame[ch, 0:3, 3:11, :] = before[:, lanes].reshape(3, 8, 128)
        nxt = after[:, lanes].reshape(3, 8, 128)
        for q in range(1, 4):
            old = frame[ch, 3 + 8 * q : 6 + 8 * q, 3:11, :]
            frame[ch, 3 + 8 * q : 6 + 8 * q, 3:11, :] = jnp.where(length == q, nxt, old)
        frame[ch, 35:38, 3:11, :] = jnp.where(length == 4, nxt, 0.0)

    def conv_half(h):
        def chunk(ch, _):
            lanes = pl.ds(pl.multiple_of(ch * 128, 128), 128)
            acc = jnp.zeros((16, 8, 128), F32)
            for i in range(7):
                for j in range(7):
                    w = dk[i, j : j + 1, lanes].reshape(1, 1, 128)
                    acc = acc + w * frame[ch, 16 * h + i : 16 * h + i + 16, j : j + 8, :]
            mixed[128 * h : 128 * h + 128, lanes] = acc.reshape(128, 128)
            return 0

        lax.fori_loop(0, CH, chunk, 0)

    conv_half(0)
    gather_relay(weight_at, s_wy, s_wx, near[:4])
    conv_half(1)
    gather_relay(weight_at, s_wy, s_wx, near[4:6])

    for q in range(4):
        rows = slice(64 * q, 64 * q + 64)
        m = mixed[rows, :]
        shifted = m - jnp.sum(m, axis=-1, keepdims=True) * (1.0 / D)
        var = jnp.sum(shifted * shifted, axis=-1, keepdims=True) * (1.0 / D)
        inv = lax.rsqrt(var + 1e-06)
        centred = shifted * inv
        mixed[rows, :] = centred
        inv_s[rows, :] = inv
        left[0, rows, :] = (centred * gain).astype(BF16)

    gather_relay(weight_at, s_wy, s_wx, near[6:])

    def take(k):
        row = row_of(k)
        arrived(wg.at[:, row, :, 1 - c], s_ws + k)
        for m in range(2):
            for col in range(NX):
                for core in range(2):
                    first = 24 * col + 12 * core
                    t96[m, first : first + 12, :] = wg[m, row, col, core].astype(F32)
            wm[m, row] = t96[m].astype(BF16)

    last = None
    for k in (0,) + near:
        row = gather_row(weight_at, s_wx, k)
        send(wg.at[:, row, :, c], wg.at[:, row, :, c], s_ws + k, (sib, o))
        if last is not None:
            take(last)
        last = k
    take(last)

    up_w = wm[0].reshape(D, HID)
    down_w = wm[1].reshape(D, HID)
    hidden = bdot(left[0], up_w) + bias1[...].reshape(1, HID)
    phi = 0.5 * (1.0 + lax.erf(hidden * INV_ROOT_TWO))
    right[1] = (hidden * phi).astype(BF16)
    grad_act = bdot(left[1], down_w)
    slope = phi + hidden * jnp.exp(-0.5 * hidden * hidden) * INV_ROOT_TAU
    right[0] = (grad_act * slope).astype(BF16)

    s_g = sem_ids(NY)
    gs[...] = bdot(left[1 - c], right[1 - c], TN_DIMS).reshape(NY, NX, RB, HID).astype(BF16)
    for k in far + (0,):
        row = lax.rem(y + k, NY)
        send(gs.at[row], grv.at[row], s_g + k, (sib, o))

    def scatter_z(value, buf, slots, s0):
        buf[...] = value.reshape(NZ, OWN_TOK, D).astype(BF16)
        for k in far:
            dest = lax.rem(o + k, NZ)
            send(buf.at[dest], slots.at[k - 1], s0 + k - 1, (t, dest))

    def scatter_z_sum(buf, slots, s0):
        total = buf[o].astype(F32)
        for k in range(1, NZ):
            arrived(slots.at[k - 1], s0 + k - 1)
            total = total + slots[k - 1].astype(F32)
        return total

    s_z = sem_ids(NZ - 1)
    s_b = sem_ids(NZ - 1)
    gf[...] = bdot(left[c], right[c], TN_DIMS).reshape(NY, NX, RB, HID)
    scatter_z(bdot(right[0], up_w, NT_DIMS), zs, zr, s_z)

    s_rx = sem_ids(3 * NY)
    s_ry = sem_ids(NY - 1)
    for k in far + (0,):
        row = lax.rem(y + k, NY)
        arrived(grv.at[row], s_g + k)
        pair = gf[row] + grv[row].astype(F32)
        gf[row] = pair
        gb[row] = pair.astype(BF16)
        for n in range(1, NX):
            col = lax.rem(x + n, NX)
            send(gb.at[row, col], rx.at[row, n - 1], s_rx + 3 * k + n - 1, (tile_at(y, col), o))
    scatter_z(bdot(right[1], down_w, NT_DIMS), bs, br, s_b)
    total = None
    for k in far + (0,):
        row = lax.rem(y + k, NY)
        total = gf[row, x]
        for n in range(1, NX):
            arrived(rx.at[row, n - 1], s_rx + 3 * k + n - 1)
            total = total + rx[row, n - 1].astype(F32)
        if k:
            ty[row] = total.astype(BF16)
            send(ty.at[row], ry.at[k - 1], s_ry + k - 1, (tile_at(row, x), o))
    for k in near:
        arrived(ry.at[k - 1], s_ry + k - 1)
        total = total + ry[k - 1].astype(F32)
    grow[...] = total
    ga[y, x] = total.astype(BF16)
    s_gy = sem_ids(NY - 1)
    s_gx = sem_ids(3 * NY)
    gather_start(grad_at, s_gy, s_gx)

    grad_normed = scatter_z_sum(zs, zr, s_z)
    own_rows = pl.ds(pl.multiple_of(o * OWN_TOK, OWN_TOK), OWN_TOK)
    own_live = length > o // 2
    centred = mixed[own_rows, :]
    g = grad_normed * gain
    mean1 = jnp.sum(g, axis=-1, keepdims=True) * (1.0 / D)
    mean2 = jnp.sum(g * centred, axis=-1, keepdims=True) * (1.0 / D)
    grad_mixed = inv_s[own_rows, :] * (g - mean1 - centred * mean2)
    grad_mixed = jnp.where(own_live, grad_mixed, 0.0)
    hg[...] = grad_mixed.astype(BF16)
    s_h = sem_ids(2)
    s_ct = sem_ids(4)
    s_ch = sem_ids(1)
    send(hg, nb.at[0], s_h, (t, lax.rem(o + 1, NZ)))
    send(hg, nb.at[1], s_h + 1, (t, lax.rem(o + NZ - 1, NZ)))
    s_c4 = sem_ids(4)

    @pl.when(first_own)
    def _():
        for q in range(4):
            pltpu.make_async_remote_copy(
                src_ref=hg, dst_ref=chd, send_sem=ss.at[s_c4 + q], recv_sem=rs.at[s_ch],
                device_id=(dn_t, 2 * q + 1), device_id_type=MESH,
            ).start()

    @pl.when(odd_own)
    def _():
        q = o // 2
        pltpu.make_async_remote_copy(
            src_ref=hg, dst_ref=ct.at[q], send_sem=ss.at[s_c4], recv_sem=rs.at[s_ct + q],
            device_id=(up_t, 0), device_id_type=MESH,
        ).start()

    frame2[...] = jnp.zeros_like(frame2)
    for ch in range(CH):
        frame2[ch, 3:7, 3:11, :] = grad_mixed[:, 128 * ch : 128 * ch + 128].reshape(4, 8, 128)

    gather_relay(grad_at, s_gy, s_gx, near[:4])

    def put_before(block):
        rows3 = block.astype(F32)[8:32]
        for ch in range(CH):
            frame2[ch, 0:3, 3:11, :] = rows3[:, 128 * ch : 128 * ch + 128].reshape(3, 8, 128)

    def put_after(block):
        rows3 = block.astype(F32)[0:24]
        for ch in range(CH):
            frame2[ch, 7:10, 3:11, :] = rows3[:, 128 * ch : 128 * ch + 128].reshape(3, 8, 128)

    gather_relay(grad_at, s_gy, s_gx, near[4:])
    arrived(nb.at[0], s_h)
    arrived(nb.at[1], s_h + 1)

    @pl.when(first_own)
    def _():
        for q in range(4):
            arrived(ct.at[q], s_ct + q)
        prev_len = lens[dn_t]
        block = ct[0].astype(F32)
        for q in range(1, 4):
            block = jnp.where(prev_len == q + 1, ct[q].astype(F32), block)
        put_before(jnp.where(t > 0, block, 0.0))
        for q in range(4):
            pltpu.make_async_remote_copy(
                src_ref=hg, dst_ref=chd, send_sem=ss.at[s_c4 + q], recv_sem=rs.at[s_ch],
                device_id=(dn_t, 2 * q + 1), device_id_type=MESH,
            ).wait_send()

    @pl.when(jnp.logical_not(first_own))
    def _():
        put_before(nb[0])

    @pl.when(odd_own)
    def _():
        arrived(chd, s_ch)
        q = o // 2
        edge = jnp.where(t < NT - 1, chd[...].astype(F32), 0.0)
        put_after(jnp.where(length == q + 1, edge, nb[1].astype(F32)))
        pltpu.make_async_remote_copy(
            src_ref=hg, dst_ref=ct.at[q], send_sem=ss.at[s_c4], recv_sem=rs.at[s_ct + q],
            device_id=(up_t, 0), device_id_type=MESH,
        ).wait_send()

    @pl.when(jnp.logical_not(odd_own))
    def _():
        put_after(nb[1])

    def chunk2(ch, _):
        lanes = pl.ds(pl.multiple_of(ch * 128, 128), 128)
        acc = jnp.zeros((4, 8, 128), F32)
        for i in range(7):
            for j in range(7):
                w = dk[6 - i, 6 - j : 7 - j, lanes].reshape(1, 1, 128)
                acc = acc + w * frame2[ch, i : i + 4, j : j + 8, :]
        res = cot[own_rows, lanes].astype(F32) + acc.reshape(OWN_TOK, 128)
        tok_ref[1, :, lanes] = jnp.where(own_live, res, 0.0).astype(BF16)
        return 0

    lax.fori_loop(0, CH, chunk2, 0)

    branch = scatter_z_sum(bs, br, s_b)
    own_keep = jnp.where(own_live, tissue[o // 2], 0).astype(F32)
    res = feat[own_rows, :].astype(F32) + (own_keep * scale) * branch
    tok_ref[0] = jnp.where(own_live, res, 0.0).astype(BF16)

    def gram_of(ks):
        for n, k in enumerate(ks):
            row = gather_row(grad_at, s_gx, k)
            gm16[n] = ga[row].astype(F32).reshape(96, HID).astype(BF16)
        g16 = gm16[0 : len(ks)].reshape(96 * len(ks), HID)
        return bdot(g16, g16, TN_DIMS)

    gram = gram_of((0,) + near[:4]) + gram_of(near[4:])
    eye = (
        lax.broadcasted_iota(jnp.int32, (HID, HID), 0) == lax.broadcasted_iota(jnp.int32, (HID, HID), 1)
    ).astype(F32)

    norm2 = jnp.sum(jnp.sum(gram * eye, axis=0, keepdims=True), axis=1, keepdims=True)
    root = lax.rsqrt(norm2 + EPS_NORM)
    gram = gram * (root * root)

    def times(a, b):
        return bdot(a.astype(BF16), b)

    def residue(a):
        a16 = a.astype(BF16)
        return (NS_B * a + NS_C * bdot(a16, a16)).astype(BF16)

    q0 = residue(gram)
    first = NS_A * gram + times(gram, q0)
    q1 = residue(NS_A * first + times(first, q0))
    ortho = grow[...] * root
    ortho = NS_A * ortho + times(ortho, q0)
    xo[c] = NS_A * ortho + times(ortho, q1)
    s_x = sem_ids(1)
    send(xo.at[c], xo.at[c], s_x, (sib, o))
    arrived(xo.at[1 - c], s_x)
    for m in range(2):
        muon_ref[m] = jnp.where(c == 0, xo[m, 0:12, :], xo[m, 12:24, :])

    for cp in sent:
        cp.wait_send()


SEMS = 160


def shards(features, cotangent, depth_kernel, ln_gain, weight_up, bias_up, weight_down, layer_scale, tissue, lengths):
    vmem = pl.BlockSpec(memory_space=pltpu.VMEM)
    hbm = pl.BlockSpec(memory_space=pltpu.HBM)
    block4 = (NY, NX, RB, HID)
    scratch = [
        pltpu.SMEM((NT,), jnp.int32),
        pltpu.SMEM((4,), jnp.int32),
        pltpu.VMEM((TOK, D), BF16),
        pltpu.VMEM((TOK, D), BF16),
        pltpu.VMEM((7, 7, D), F32),
        pltpu.VMEM((D,), F32),
        pltpu.VMEM((HID,), F32),
        pltpu.VMEM((D,), F32),
        pltpu.VMEM((2, 96, HID), F32),
        pltpu.VMEM((2, NY, NX, 2, 12, HID), BF16),
        pltpu.VMEM((2, NY, 96, HID), BF16),
        pltpu.VMEM((2, 24, D), BF16),
        pltpu.VMEM((2, 24, D), BF16),
        pltpu.VMEM((CH, 38, 16, 128), F32),
        pltpu.VMEM((TOK, D), F32),
        pltpu.VMEM((TOK, 1), F32),
        pltpu.VMEM((2, TOK, D), BF16),
        pltpu.VMEM((2, TOK, HID), BF16),
        pltpu.VMEM((NZ, OWN_TOK, D), BF16),
        pltpu.VMEM((NZ - 1, OWN_TOK, D), BF16),
        pltpu.VMEM((NZ, OWN_TOK, D), BF16),
        pltpu.VMEM((NZ - 1, OWN_TOK, D), BF16),
        pltpu.VMEM(block4, BF16),
        pltpu.VMEM(block4, BF16),
        pltpu.VMEM(block4, F32),
        pltpu.VMEM(block4, BF16),
        pltpu.VMEM((NY, NX - 1, RB, HID), BF16),
        pltpu.VMEM((NY, RB, HID), BF16),
        pltpu.VMEM((NY - 1, RB, HID), BF16),
        pltpu.VMEM((RB, HID), F32),
        pltpu.VMEM(block4, BF16),
        pltpu.VMEM((NY, 96, HID), BF16),
        pltpu.VMEM((OWN_TOK, D), BF16),
        pltpu.VMEM((2, OWN_TOK, D), BF16),
        pltpu.VMEM((4, OWN_TOK, D), BF16),
        pltpu.VMEM((OWN_TOK, D), BF16),
        pltpu.VMEM((CH, 10, 16, 128), F32),
        pltpu.VMEM((2, RB, HID), F32),
        pltpu.SemaphoreType.DMA((SEMS,)),
        pltpu.SemaphoreType.DMA((SEMS,)),
        pltpu.SemaphoreType.DMA((10,)),
    ]
    outs = pl.pallas_call(
        body,
        out_shape=(
            jax.ShapeDtypeStruct((2, OWN_TOK, D), BF16),
            jax.ShapeDtypeStruct((2, 12, HID), F32),
        ),
        in_specs=[hbm] * 10,
        out_specs=(vmem,) * 2,
        scratch_shapes=scratch,
        compiler_params=pltpu.CompilerParams(
            collective_id=0, has_side_effects=True, vmem_limit_bytes=62 << 20
        ),
    )(
        lengths,
        tissue.reshape(4),
        features.reshape(TOK, D),
        cotangent.reshape(TOK, D),
        depth_kernel,
        ln_gain,
        weight_up,
        bias_up,
        weight_down.T,
        layer_scale,
    )
    tokens, muon = outs
    return (
        tokens[0].reshape(4, 8, D),
        tokens[1].reshape(4, 8, D),
        muon[0],
        muon[1].T,
    )


def solution(mesh):
    in_specs = (
        P("tile", None, None),
        P("tile", None, None),
        P(),
        P(),
        P("tile", "own"),
        P("own"),
        P("own", "tile"),
        P(),
        P("tile", None),
        P(),
    )
    out_specs = (
        P(("tile", "own"), None, None),
        P(("tile", "own"), None, None),
        P("tile", "own"),
        P("own", "tile"),
    )
    return jax.shard_map(shards, mesh=mesh, in_specs=in_specs, out_specs=out_specs, check_vma=False)
```

```python
import jax
import jax.numpy as jnp
from jax import lax
from jax.experimental import pallas as pl
from jax.experimental.pallas import tpu as pltpu
from jax.sharding import PartitionSpec as P

MESH = pl.DeviceIdType.MESH
F32 = jnp.float32
BF16 = jnp.bfloat16

NY, NX, NZ = 8, 4, 8
NT = NY * NX * 2
D = 768
HID = 384
TOK = 256
CH = D // 128
RB = 24
OWN_TOK = 32

INV_ROOT_TWO = 0.7071067811865476
INV_ROOT_TAU = 0.3989422804014327
NS_A = 3.4445
NS_B = -4.775
NS_C = 2.0315
EPS_NORM = 1e-06


def bdot(a, b, dims=(((1,), (0,)), ((), ()))):
    return lax.dot_general(a, b, dims, preferred_element_type=F32)


NT_DIMS = (((1,), (1,)), ((), ()))
TN_DIMS = (((0,), (0,)), ((), ()))


def body(
    lens_h, tissue_h, feat_h, cot_h, dk_h, gain_h, wu_h, bias_h, wd_h, scale_h,
    tok_ref, muon_ref,
    lens, tissue, feat, cot, dk, gain1, bias1, scale1, pieces, piece_in, t24, wg, wm, rim, halo, frame, mixed, inv_s, left, right,
    zs, zr, bs, br, gs, grv, gf, gb, rx, ty, ry, grow, ga, gm16, hg, nb, ct, chd, frame2, xo,
    ss, rs, ls,
):
    t = lax.axis_index("tile")
    o = lax.axis_index("own")
    c = lax.rem(t, 2)
    chip = t // 2
    x = lax.rem(chip, NX)
    y = chip // NX
    sib = t + 1 - 2 * c

    def tile_at(yy, xx):
        return (yy * NX + xx) * 2 + c

    counter = [0]
    sent = []

    def sem_ids(n):
        first = counter[0]
        counter[0] += n
        return first

    def copy(src, dst, sem, dev):
        return pltpu.make_async_remote_copy(
            src_ref=src, dst_ref=dst, send_sem=ss.at[sem], recv_sem=rs.at[sem],
            device_id=dev, device_id_type=MESH,
        )

    def send(src, dst, sem, dev):
        cp = copy(src, dst, sem, dev)
        cp.start()
        sent.append(cp)

    def arrived(dst, sem):
        copy(dst, dst, sem, (t, o)).wait_recv()

    fetches = {}
    for n, (name, src, dst) in enumerate(
        (
            ("wu", wu_h, pieces.at[0]), ("wd", wd_h, pieces.at[1]), ("lens", lens_h, lens),
            ("feat", feat_h, feat), ("tissue", tissue_h, tissue), ("dk", dk_h, dk), ("gain", gain_h, gain1),
            ("scale", scale_h, scale1), ("cot", cot_h, cot), ("bias", bias_h, bias1),
        )
    ):
        fetches[name] = pltpu.make_async_copy(src, dst, ls.at[n])
        fetches[name].start()

    bar = pltpu.get_barrier_semaphore()

    def greet(dev):
        pl.semaphore_signal(bar, inc=1, device_id=dev, device_id_type=MESH)

    up_t = lax.rem(t + 1, NT)
    dn_t = lax.rem(t + NT - 1, NT)
    greet((sib, o))
    for k in range(1, NY):
        greet((tile_at(lax.rem(y + k, NY), x), o))
    for k in range(1, NX):
        greet((tile_at(y, lax.rem(x + k, NX)), o))
    for k in range(1, NZ):
        greet((t, lax.rem(o + k, NZ)))
    greet((up_t, o))
    greet((dn_t, o))
    first_own = o == 0
    odd_own = lax.rem(o, 2) == 1

    @pl.when(first_own)
    def _():
        for q in range(4):
            greet((dn_t, 2 * q + 1))

    @pl.when(odd_own)
    def _():
        greet((up_t, 0))

    expected = 1 + (NY - 1) + (NX - 1) + (NZ - 1) + 2
    fetches["wu"].wait()
    fetches["wd"].wait()
    pl.semaphore_wait(bar, expected + 4 * ((NZ - o) // NZ) + lax.rem(o, 2))

    s_piece = sem_ids(1)
    send(pieces.at[1 - c], piece_in, s_piece, (sib, o))

    near = (1, 7, 2, 6, 3, 5, 4)
    far = near[::-1]

    def row_of(k):
        return lax.rem(y + NY - k, NY)

    def share_x(at, row, sem):
        for k in range(1, NX):
            send(at(row, x), at(row, x), sem + k - 1, (tile_at(y, lax.rem(x + k, NX)), o))

    def gather_start(at, s_y, s_x):
        for k in far:
            send(at(y, x), at(y, x), s_y + k - 1, (tile_at(lax.rem(y + k, NY), x), o))
        share_x(at, y, s_x)

    def gather_relay(at, s_y, s_x, ks):
        for k in ks:
            row = row_of(k)
            arrived(at(row, x), s_y + k - 1)
            share_x(at, row, s_x + 3 * k)

    def gather_row(at, s_x, k):
        row = row_of(k)
        for n in range(1, NX):
            arrived(at(row, lax.rem(x + NX - n, NX)), s_x + 3 * k + n - 1)
        return row

    def weight_at(row, col):
        return wg.at[c, row, col]

    def grad_at(row, col):
        return ga.at[row, col]

    s_wy = sem_ids(NY - 1)
    s_wx = sem_ids(3 * NY)
    s_ws = sem_ids(NY)
    fetches["lens"].wait()
    fetches["feat"].wait()
    length = lens[t]
    rim[0] = feat[0:24, :].astype(F32).astype(BF16)
    tail = feat[0:64, :].astype(F32)[40:64]
    for q in range(1, 4):
        tail = jnp.where(length == q + 1, feat[64 * q : 64 * q + 64, :].astype(F32)[40:64], tail)
    rim[1] = tail.astype(BF16)
    s_halo = sem_ids(2)
    send(rim.at[1], halo.at[0], s_halo, (up_t, o))
    send(rim.at[0], halo.at[1], s_halo + 1, (dn_t, o))

    arrived(piece_in, s_piece)
    mine = pieces[c].astype(F32)
    other = piece_in[...].astype(F32)
    t24[0:12, :] = jnp.where(c == 0, mine, other)
    t24[12:24, :] = jnp.where(c == 0, other, mine)
    wg[c, y, x] = t24[...].astype(BF16)
    gather_start(weight_at, s_wy, s_wx)

    for name in ("tissue", "dk", "gain", "scale", "cot", "bias"):
        fetches[name].wait()
    gain = gain1[...].reshape(1, D)
    scale = scale1[...].reshape(1, D)
    frame[...] = jnp.zeros_like(frame)
    for q in range(4):
        rows = slice(64 * q, 64 * q + 64)
        live = length > q
        keep = jnp.where(live, tissue[q], 0).astype(F32)
        f = feat[rows, :].astype(F32)
        if q:
            f = jnp.where(live, f, 0.0)
        for ch in range(CH):
            frame[ch, 3 + 8 * q : 11 + 8 * q, 3:11, :] = f[:, 128 * ch : 128 * ch + 128].reshape(8, 8, 128)
        left[1, rows, :] = ((keep * scale) * cot[rows, :].astype(F32)).astype(BF16)

    arrived(halo.at[0], s_halo)
    arrived(halo.at[1], s_halo + 1)
    before = jnp.where(t > 0, halo[0].astype(F32), 0.0)
    after = jnp.where(t < NT - 1, halo[1].astype(F32), 0.0)
    for ch in range(CH):
        lanes = slice(128 * ch, 128 * ch + 128)
        frame[ch, 0:3, 3:11, :] = before[:, lanes].reshape(3, 8, 128)
        nxt = after[:, lanes].reshape(3, 8, 128)
        for q in range(1, 4):
            old = frame[ch, 3 + 8 * q : 6 + 8 * q, 3:11, :]
            frame[ch, 3 + 8 * q : 6 + 8 * q, 3:11, :] = jnp.where(length == q, nxt, old)
        frame[ch, 35:38, 3:11, :] = jnp.where(length == 4, nxt, 0.0)

    def conv_half(h):
        def chunk(ch, _):
            lanes = pl.ds(pl.multiple_of(ch * 128, 128), 128)
            acc = jnp.zeros((16, 8, 128), F32)
            for i in range(7):
                for j in range(7):
                    w = dk[i, j : j + 1, lanes].reshape(1, 1, 128)
                    acc = acc + w * frame[ch, 16 * h + i : 16 * h + i + 16, j : j + 8, :]
            mixed[128 * h : 128 * h + 128, lanes] = acc.reshape(128, 128)
            return 0

        lax.fori_loop(0, CH, chunk, 0)

    conv_half(0)
    gather_relay(weight_at, s_wy, s_wx, near[:4])
    conv_half(1)
    gather_relay(weight_at, s_wy, s_wx, near[4:6])

    for q in range(4):
        rows = slice(64 * q, 64 * q + 64)
        m = mixed[rows, :]
        shifted = m - jnp.sum(m, axis=-1, keepdims=True) * (1.0 / D)
        var = jnp.sum(shifted * shifted, axis=-1, keepdims=True) * (1.0 / D)
        inv = lax.rsqrt(var + 1e-06)
        centred = shifted * inv
        mixed[rows, :] = centred
        inv_s[rows, :] = inv
        left[0, rows, :] = (centred * gain).astype(BF16)

    gather_relay(weight_at, s_wy, s_wx, near[6:])

    def take(m, k):
        wm[m, row_of(k)] = wg[m, row_of(k)].astype(F32).reshape(96, HID).astype(BF16)

    def take_other(k):
        arrived(wg.at[1 - c, row_of(k)], s_ws + k)
        take(1 - c, k)

    last = None
    for k in (0,) + near:
        row = gather_row(weight_at, s_wx, k)
        send(wg.at[c, row], wg.at[c, row], s_ws + k, (sib, o))
        take(c, k)
        if last is not None:
            take_other(last)
        last = k
    take_other(last)

    up_w = wm[0].reshape(D, HID)
    down_w = wm[1].reshape(D, HID)
    hidden = bdot(left[0], up_w) + bias1[...].reshape(1, HID)
    phi = 0.5 * (1.0 + lax.erf(hidden * INV_ROOT_TWO))
    right[1] = (hidden * phi).astype(BF16)
    grad_act = bdot(left[1], down_w)
    slope = phi + hidden * jnp.exp(-0.5 * hidden * hidden) * INV_ROOT_TAU
    right[0] = (grad_act * slope).astype(BF16)

    s_g = sem_ids(NY)
    gs[...] = bdot(left[1 - c], right[1 - c], TN_DIMS).reshape(NY, NX, RB, HID).astype(BF16)
    for k in far + (0,):
        row = lax.rem(y + k, NY)
        send(gs.at[row], grv.at[row], s_g + k, (sib, o))

    def scatter_z(value, buf, slots, s0):
        buf[...] = value.reshape(NZ, OWN_TOK, D).astype(BF16)
        for k in far:
            dest = lax.rem(o + k, NZ)
            send(buf.at[dest], slots.at[k - 1], s0 + k - 1, (t, dest))

    def scatter_z_sum(buf, slots, s0):
        total = buf[o].astype(F32)
        for k in range(1, NZ):
            arrived(slots.at[k - 1], s0 + k - 1)
            total = total + slots[k - 1].astype(F32)
        return total

    s_z = sem_ids(NZ - 1)
    s_b = sem_ids(NZ - 1)
    gf[...] = bdot(left[c], right[c], TN_DIMS).reshape(NY, NX, RB, HID)
    scatter_z(bdot(right[0], up_w, NT_DIMS), zs, zr, s_z)

    s_rx = sem_ids(3 * NY)
    s_ry = sem_ids(NY - 1)
    for k in far + (0,):
        row = lax.rem(y + k, NY)
        arrived(grv.at[row], s_g + k)
        pair = gf[row] + grv[row].astype(F32)
        gf[row] = pair
        gb[row] = pair.astype(BF16)
        for n in range(1, NX):
            col = lax.rem(x + n, NX)
            send(gb.at[row, col], rx.at[row, n - 1], s_rx + 3 * k + n - 1, (tile_at(y, col), o))
    scatter_z(bdot(right[1], down_w, NT_DIMS), bs, br, s_b)
    total = None
    for k in far + (0,):
        row = lax.rem(y + k, NY)
        total = gf[row, x]
        for n in range(1, NX):
            arrived(rx.at[row, n - 1], s_rx + 3 * k + n - 1)
            total = total + rx[row, n - 1].astype(F32)
        if k:
            ty[row] = total.astype(BF16)
            send(ty.at[row], ry.at[k - 1], s_ry + k - 1, (tile_at(row, x), o))
    for k in near:
        arrived(ry.at[k - 1], s_ry + k - 1)
        total = total + ry[k - 1].astype(F32)
    grow[...] = total
    ga[y, x] = total.astype(BF16)
    s_gy = sem_ids(NY - 1)
    s_gx = sem_ids(3 * NY)
    gather_start(grad_at, s_gy, s_gx)

    gather_relay(grad_at, s_gy, s_gx, near[:4])

    grad_normed = scatter_z_sum(zs, zr, s_z)
    own_rows = pl.ds(pl.multiple_of(o * OWN_TOK, OWN_TOK), OWN_TOK)
    own_live = length > o // 2
    centred = mixed[own_rows, :]
    g = grad_normed * gain
    mean1 = jnp.sum(g, axis=-1, keepdims=True) * (1.0 / D)
    mean2 = jnp.sum(g * centred, axis=-1, keepdims=True) * (1.0 / D)
    grad_mixed = inv_s[own_rows, :] * (g - mean1 - centred * mean2)
    grad_mixed = jnp.where(own_live, grad_mixed, 0.0)
    hg[...] = grad_mixed.astype(BF16)
    s_h = sem_ids(2)
    s_ct = sem_ids(4)
    s_ch = sem_ids(1)
    send(hg, nb.at[0], s_h, (t, lax.rem(o + 1, NZ)))
    send(hg, nb.at[1], s_h + 1, (t, lax.rem(o + NZ - 1, NZ)))
    s_c4 = sem_ids(4)

    @pl.when(first_own)
    def _():
        for q in range(4):
            pltpu.make_async_remote_copy(
                src_ref=hg, dst_ref=chd, send_sem=ss.at[s_c4 + q], recv_sem=rs.at[s_ch],
                device_id=(dn_t, 2 * q + 1), device_id_type=MESH,
            ).start()

    @pl.when(odd_own)
    def _():
        q = o // 2
        pltpu.make_async_remote_copy(
            src_ref=hg, dst_ref=ct.at[q], send_sem=ss.at[s_c4], recv_sem=rs.at[s_ct + q],
            device_id=(up_t, 0), device_id_type=MESH,
        ).start()

    frame2[...] = jnp.zeros_like(frame2)
    for ch in range(CH):
        frame2[ch, 3:7, 3:11, :] = grad_mixed[:, 128 * ch : 128 * ch + 128].reshape(4, 8, 128)

    gather_relay(grad_at, s_gy, s_gx, near[4:])

    def gram_of(ks):
        for n, k in enumerate(ks):
            row = gather_row(grad_at, s_gx, k)
            gm16[n] = ga[row].astype(F32).reshape(96, HID).astype(BF16)
        g16 = gm16[0 : len(ks)].reshape(96 * len(ks), HID)
        return bdot(g16, g16, TN_DIMS)

    gram = gram_of((0,) + near[:4]) + gram_of(near[4:])
    eye = (
        lax.broadcasted_iota(jnp.int32, (HID, HID), 0) == lax.broadcasted_iota(jnp.int32, (HID, HID), 1)
    ).astype(F32)

    norm2 = jnp.sum(jnp.sum(gram * eye, axis=0, keepdims=True), axis=1, keepdims=True)
    root = lax.rsqrt(norm2 + EPS_NORM)
    gram = gram * (root * root)

    def times(a, b):
        return bdot(a.astype(BF16), b)

    def residue(a):
        a16 = a.astype(BF16)
        return (NS_B * a + NS_C * bdot(a16, a16)).astype(BF16)

    q0 = residue(gram)
    first = NS_A * gram + times(gram, q0)
    q1 = residue(NS_A * first + times(first, q0))
    ortho = grow[...] * root
    ortho = NS_A * ortho + times(ortho, q0)
    xo[c] = NS_A * ortho + times(ortho, q1)
    s_x = sem_ids(1)
    send(xo.at[c], xo.at[c], s_x, (sib, o))
    def put_before(block):
        rows3 = block.astype(F32)[8:32]
        for ch in range(CH):
            frame2[ch, 0:3, 3:11, :] = rows3[:, 128 * ch : 128 * ch + 128].reshape(3, 8, 128)

    def put_after(block):
        rows3 = block.astype(F32)[0:24]
        for ch in range(CH):
            frame2[ch, 7:10, 3:11, :] = rows3[:, 128 * ch : 128 * ch + 128].reshape(3, 8, 128)

    arrived(nb.at[0], s_h)
    arrived(nb.at[1], s_h + 1)

    @pl.when(first_own)
    def _():
        for q in range(4):
            arrived(ct.at[q], s_ct + q)
        prev_len = lens[dn_t]
        block = ct[0].astype(F32)
        for q in range(1, 4):
            block = jnp.where(prev_len == q + 1, ct[q].astype(F32), block)
        put_before(jnp.where(t > 0, block, 0.0))
        for q in range(4):
            pltpu.make_async_remote_copy(
                src_ref=hg, dst_ref=chd, send_sem=ss.at[s_c4 + q], recv_sem=rs.at[s_ch],
                device_id=(dn_t, 2 * q + 1), device_id_type=MESH,
            ).wait_send()

    @pl.when(jnp.logical_not(first_own))
    def _():
        put_before(nb[0])

    @pl.when(odd_own)
    def _():
        arrived(chd, s_ch)
        q = o // 2
        edge = jnp.where(t < NT - 1, chd[...].astype(F32), 0.0)
        put_after(jnp.where(length == q + 1, edge, nb[1].astype(F32)))
        pltpu.make_async_remote_copy(
            src_ref=hg, dst_ref=ct.at[q], send_sem=ss.at[s_c4], recv_sem=rs.at[s_ct + q],
            device_id=(up_t, 0), device_id_type=MESH,
        ).wait_send()

    @pl.when(jnp.logical_not(odd_own))
    def _():
        put_after(nb[1])

    def chunk2(ch, _):
        lanes = pl.ds(pl.multiple_of(ch * 128, 128), 128)
        acc = jnp.zeros((4, 8, 128), F32)
        for i in range(7):
            for j in range(7):
                w = dk[6 - i, 6 - j : 7 - j, lanes].reshape(1, 1, 128)
                acc = acc + w * frame2[ch, i : i + 4, j : j + 8, :]
        res = cot[own_rows, lanes].astype(F32) + acc.reshape(OWN_TOK, 128)
        tok_ref[1, :, lanes] = jnp.where(own_live, res, 0.0).astype(BF16)
        return 0

    lax.fori_loop(0, CH, chunk2, 0)

    branch = scatter_z_sum(bs, br, s_b)
    own_keep = jnp.where(own_live, tissue[o // 2], 0).astype(F32)
    res = feat[own_rows, :].astype(F32) + (own_keep * scale) * branch
    tok_ref[0] = jnp.where(own_live, res, 0.0).astype(BF16)

    arrived(xo.at[1 - c], s_x)
    for m in range(2):
        muon_ref[m] = jnp.where(c == 0, xo[m, 0:12, :], xo[m, 12:24, :])

    for cp in sent:
        cp.wait_send()


SEMS = 160


def shards(features, cotangent, depth_kernel, ln_gain, weight_up, bias_up, weight_down, layer_scale, tissue, lengths):
    vmem = pl.BlockSpec(memory_space=pltpu.VMEM)
    hbm = pl.BlockSpec(memory_space=pltpu.HBM)
    block4 = (NY, NX, RB, HID)
    scratch = [
        pltpu.SMEM((NT,), jnp.int32),
        pltpu.SMEM((4,), jnp.int32),
        pltpu.VMEM((TOK, D), BF16),
        pltpu.VMEM((TOK, D), BF16),
        pltpu.VMEM((7, 7, D), F32),
        pltpu.VMEM((D,), F32),
        pltpu.VMEM((HID,), F32),
        pltpu.VMEM((D,), F32),
        pltpu.VMEM((2, 12, HID), BF16),
        pltpu.VMEM((12, HID), BF16),
        pltpu.VMEM((24, HID), F32),
        pltpu.VMEM((2,) + block4, BF16),
        pltpu.VMEM((2, NY, 96, HID), BF16),
        pltpu.VMEM((2, 24, D), BF16),
        pltpu.VMEM((2, 24, D), BF16),
        pltpu.VMEM((CH, 38, 16, 128), F32),
        pltpu.VMEM((TOK, D), F32),
        pltpu.VMEM((TOK, 1), F32),
        pltpu.VMEM((2, TOK, D), BF16),
        pltpu.VMEM((2, TOK, HID), BF16),
        pltpu.VMEM((NZ, OWN_TOK, D), BF16),
        pltpu.VMEM((NZ - 1, OWN_TOK, D), BF16),
        pltpu.VMEM((NZ, OWN_TOK, D), BF16),
        pltpu.VMEM((NZ - 1, OWN_TOK, D), BF16),
        pltpu.VMEM(block4, BF16),
        pltpu.VMEM(block4, BF16),
        pltpu.VMEM(block4, F32),
        pltpu.VMEM(block4, BF16),
        pltpu.VMEM((NY, NX - 1, RB, HID), BF16),
        pltpu.VMEM((NY, RB, HID), BF16),
        pltpu.VMEM((NY - 1, RB, HID), BF16),
        pltpu.VMEM((RB, HID), F32),
        pltpu.VMEM(block4, BF16),
        pltpu.VMEM((NY, 96, HID), BF16),
        pltpu.VMEM((OWN_TOK, D), BF16),
        pltpu.VMEM((2, OWN_TOK, D), BF16),
        pltpu.VMEM((4, OWN_TOK, D), BF16),
        pltpu.VMEM((OWN_TOK, D), BF16),
        pltpu.VMEM((CH, 10, 16, 128), F32),
        pltpu.VMEM((2, RB, HID), F32),
        pltpu.SemaphoreType.DMA((SEMS,)),
        pltpu.SemaphoreType.DMA((SEMS,)),
        pltpu.SemaphoreType.DMA((10,)),
    ]
    outs = pl.pallas_call(
        body,
        out_shape=(
            jax.ShapeDtypeStruct((2, OWN_TOK, D), BF16),
            jax.ShapeDtypeStruct((2, 12, HID), F32),
        ),
        in_specs=[hbm] * 10,
        out_specs=(vmem,) * 2,
        scratch_shapes=scratch,
        compiler_params=pltpu.CompilerParams(
            collective_id=0, has_side_effects=True, vmem_limit_bytes=62 << 20
        ),
    )(
        lengths,
        tissue.reshape(4),
        features.reshape(TOK, D),
        cotangent.reshape(TOK, D),
        depth_kernel,
        ln_gain,
        weight_up,
        bias_up,
        weight_down.T,
        layer_scale,
    )
    tokens, muon = outs
    return (
        tokens[0].reshape(4, 8, D),
        tokens[1].reshape(4, 8, D),
        muon[0],
        muon[1].T,
    )


def solution(mesh):
    in_specs = (
        P("tile", None, None),
        P("tile", None, None),
        P(),
        P(),
        P("tile", "own"),
        P("own"),
        P("own", "tile"),
        P(),
        P("tile", None),
        P(),
    )
    out_specs = (
        P(("tile", "own"), None, None),
        P(("tile", "own"), None, None),
        P("tile", "own"),
        P("own", "tile"),
    )
    return jax.shard_map(shards, mesh=mesh, in_specs=in_specs, out_specs=out_specs, check_vma=False)
```

```python
import jax
import jax.numpy as jnp
from jax import lax
from jax.experimental import pallas as pl
from jax.experimental.pallas import tpu as pltpu
from jax.sharding import PartitionSpec as P

MESH = pl.DeviceIdType.MESH
F32 = jnp.float32
BF16 = jnp.bfloat16

NY, NX, NZ = 8, 4, 8
NT = NY * NX * 2
D = 768
HID = 384
TOK = 256
CH = D // 128
RB = 24
OWN_TOK = 32

INV_ROOT_TWO = 0.7071067811865476
INV_ROOT_TAU = 0.3989422804014327
NS_A = 3.4445
NS_B = -4.775
NS_C = 2.0315
EPS_NORM = 1e-06


def bdot(a, b, dims=(((1,), (0,)), ((), ()))):
    return lax.dot_general(a, b, dims, preferred_element_type=F32)


NT_DIMS = (((1,), (1,)), ((), ()))
TN_DIMS = (((0,), (0,)), ((), ()))


def body(
    lens_h, tissue_h, feat_h, cot_h, dk_h, gain_h, wu_h, bias_h, wd_h, scale_h,
    tok_ref, muon_ref,
    lens, tissue, feat, cot, dk, gain1, bias1, scale1, pieces, piece_in, t24, wg, wm, rim, halo, frame, mixed, inv_s, left, right,
    zs, zr, bs, br, left_in, right_in, gf, gb, rx, ty, ry, grow, ga, gm16, hg, nb, ct, chd, frame2, xo,
    ss, rs, ls,
):
    t = lax.axis_index("tile")
    o = lax.axis_index("own")
    c = lax.rem(t, 2)
    chip = t // 2
    x = lax.rem(chip, NX)
    y = chip // NX
    sib = t + 1 - 2 * c

    def tile_at(yy, xx):
        return (yy * NX + xx) * 2 + c

    counter = [0]
    sent = []

    def sem_ids(n):
        first = counter[0]
        counter[0] += n
        return first

    def copy(src, dst, sem, dev):
        return pltpu.make_async_remote_copy(
            src_ref=src, dst_ref=dst, send_sem=ss.at[sem], recv_sem=rs.at[sem],
            device_id=dev, device_id_type=MESH,
        )

    def send(src, dst, sem, dev):
        cp = copy(src, dst, sem, dev)
        cp.start()
        sent.append(cp)

    def arrived(dst, sem):
        copy(dst, dst, sem, (t, o)).wait_recv()

    fetches = {}
    for n, (name, src, dst) in enumerate(
        (
            ("wu", wu_h, pieces.at[0]), ("wd", wd_h, pieces.at[1]), ("lens", lens_h, lens),
            ("feat", feat_h, feat), ("tissue", tissue_h, tissue), ("dk", dk_h, dk), ("gain", gain_h, gain1),
            ("scale", scale_h, scale1), ("cot", cot_h, cot), ("bias", bias_h, bias1),
        )
    ):
        fetches[name] = pltpu.make_async_copy(src, dst, ls.at[n])
        fetches[name].start()

    bar = pltpu.get_barrier_semaphore()

    def greet(dev):
        pl.semaphore_signal(bar, inc=1, device_id=dev, device_id_type=MESH)

    up_t = lax.rem(t + 1, NT)
    dn_t = lax.rem(t + NT - 1, NT)
    greet((sib, o))
    for k in range(1, NY):
        greet((tile_at(lax.rem(y + k, NY), x), o))
    for k in range(1, NX):
        greet((tile_at(y, lax.rem(x + k, NX)), o))
    for k in range(1, NZ):
        greet((t, lax.rem(o + k, NZ)))
    greet((up_t, o))
    greet((dn_t, o))
    first_own = o == 0
    odd_own = lax.rem(o, 2) == 1

    @pl.when(first_own)
    def _():
        for q in range(4):
            greet((dn_t, 2 * q + 1))

    @pl.when(odd_own)
    def _():
        greet((up_t, 0))

    expected = 1 + (NY - 1) + (NX - 1) + (NZ - 1) + 2
    fetches["wu"].wait()
    fetches["wd"].wait()
    pl.semaphore_wait(bar, expected + 4 * ((NZ - o) // NZ) + lax.rem(o, 2))

    s_piece = sem_ids(1)
    send(pieces.at[1 - c], piece_in, s_piece, (sib, o))

    near = (1, 7, 2, 6, 3, 5, 4)
    far = near[::-1]

    def row_of(k):
        return lax.rem(y + NY - k, NY)

    def share_x(at, row, sem):
        for k in range(1, NX):
            send(at(row, x), at(row, x), sem + k - 1, (tile_at(y, lax.rem(x + k, NX)), o))

    def gather_start(at, s_y, s_x):
        for k in near:
            send(at(y, x), at(y, x), s_y + k - 1, (tile_at(lax.rem(y + k, NY), x), o))
        share_x(at, y, s_x)

    def gather_relay(at, s_y, s_x, ks):
        for k in ks:
            row = row_of(k)
            arrived(at(row, x), s_y + k - 1)
            share_x(at, row, s_x + 3 * k)

    def gather_row(at, s_x, k):
        row = row_of(k)
        for n in range(1, NX):
            arrived(at(row, lax.rem(x + NX - n, NX)), s_x + 3 * k + n - 1)
        return row

    def weight_at(row, col):
        return wg.at[c, row, col]

    def grad_at(row, col):
        return ga.at[row, col]

    s_wy = sem_ids(NY - 1)
    s_wx = sem_ids(3 * NY)
    s_ws = sem_ids(NY)
    fetches["lens"].wait()
    fetches["feat"].wait()
    length = lens[t]
    rim[0] = feat[0:24, :].astype(F32).astype(BF16)
    tail = feat[0:64, :].astype(F32)[40:64]
    for q in range(1, 4):
        tail = jnp.where(length == q + 1, feat[64 * q : 64 * q + 64, :].astype(F32)[40:64], tail)
    rim[1] = tail.astype(BF16)
    s_halo = sem_ids(2)
    send(rim.at[1], halo.at[0], s_halo, (up_t, o))
    send(rim.at[0], halo.at[1], s_halo + 1, (dn_t, o))

    arrived(piece_in, s_piece)
    mine = pieces[c].astype(F32)
    other = piece_in[...].astype(F32)
    t24[0:12, :] = jnp.where(c == 0, mine, other)
    t24[12:24, :] = jnp.where(c == 0, other, mine)
    wg[c, y, x] = t24[...].astype(BF16)
    gather_start(weight_at, s_wy, s_wx)

    for name in ("tissue", "dk", "gain", "scale", "cot", "bias"):
        fetches[name].wait()
    gain = gain1[...].reshape(1, D)
    scale = scale1[...].reshape(1, D)
    frame[...] = jnp.zeros_like(frame)
    for q in range(4):
        rows = slice(64 * q, 64 * q + 64)
        live = length > q
        keep = jnp.where(live, tissue[q], 0).astype(F32)
        f = feat[rows, :].astype(F32)
        if q:
            f = jnp.where(live, f, 0.0)
        for ch in range(CH):
            frame[ch, 3 + 8 * q : 11 + 8 * q, 3:11, :] = f[:, 128 * ch : 128 * ch + 128].reshape(8, 8, 128)
        left[1, rows, :] = ((keep * scale) * cot[rows, :].astype(F32)).astype(BF16)

    arrived(halo.at[0], s_halo)
    arrived(halo.at[1], s_halo + 1)
    before = jnp.where(t > 0, halo[0].astype(F32), 0.0)
    after = jnp.where(t < NT - 1, halo[1].astype(F32), 0.0)
    for ch in range(CH):
        lanes = slice(128 * ch, 128 * ch + 128)
        frame[ch, 0:3, 3:11, :] = before[:, lanes].reshape(3, 8, 128)
        nxt = after[:, lanes].reshape(3, 8, 128)
        for q in range(1, 4):
            old = frame[ch, 3 + 8 * q : 6 + 8 * q, 3:11, :]
            frame[ch, 3 + 8 * q : 6 + 8 * q, 3:11, :] = jnp.where(length == q, nxt, old)
        frame[ch, 35:38, 3:11, :] = jnp.where(length == 4, nxt, 0.0)

    def conv_half(h):
        def chunk(ch, _):
            lanes = pl.ds(pl.multiple_of(ch * 128, 128), 128)
            acc = jnp.zeros((16, 8, 128), F32)
            for i in range(7):
                for j in range(7):
                    w = dk[i, j : j + 1, lanes].reshape(1, 1, 128)
                    acc = acc + w * frame[ch, 16 * h + i : 16 * h + i + 16, j : j + 8, :]
            mixed[128 * h : 128 * h + 128, lanes] = acc.reshape(128, 128)
            return 0

        lax.fori_loop(0, CH, chunk, 0)

    conv_half(0)
    gather_relay(weight_at, s_wy, s_wx, near[:4])
    conv_half(1)
    gather_relay(weight_at, s_wy, s_wx, near[4:6])

    for q in range(4):
        rows = slice(64 * q, 64 * q + 64)
        m = mixed[rows, :]
        shifted = m - jnp.sum(m, axis=-1, keepdims=True) * (1.0 / D)
        var = jnp.sum(shifted * shifted, axis=-1, keepdims=True) * (1.0 / D)
        inv = lax.rsqrt(var + 1e-06)
        centred = shifted * inv
        mixed[rows, :] = centred
        inv_s[rows, :] = inv
        left[0, rows, :] = (centred * gain).astype(BF16)

    gather_relay(weight_at, s_wy, s_wx, near[6:])
    s_l = sem_ids(2)
    send(left.at[1 - c], left_in, s_l, (sib, o))

    def take(m, k):
        wm[m, row_of(k)] = wg[m, row_of(k)].astype(F32).reshape(96, HID).astype(BF16)

    def take_other(k):
        arrived(wg.at[1 - c, row_of(k)], s_ws + k)
        take(1 - c, k)

    last = None
    for k in (0,) + near:
        row = gather_row(weight_at, s_wx, k)
        send(wg.at[c, row], wg.at[c, row], s_ws + k, (sib, o))
        take(c, k)
        if last is not None:
            take_other(last)
        last = k
    take_other(last)

    up_w = wm[0].reshape(D, HID)
    down_w = wm[1].reshape(D, HID)
    hidden = bdot(left[0], up_w) + bias1[...].reshape(1, HID)
    phi = 0.5 * (1.0 + lax.erf(hidden * INV_ROOT_TWO))
    right[1] = (hidden * phi).astype(BF16)
    grad_act = bdot(left[1], down_w)
    slope = phi + hidden * jnp.exp(-0.5 * hidden * hidden) * INV_ROOT_TAU
    right[0] = (grad_act * slope).astype(BF16)

    send(right.at[1 - c], right_in, s_l + 1, (sib, o))

    def scatter_z(value, buf, slots, s0):
        buf[...] = value.reshape(NZ, OWN_TOK, D).astype(BF16)
        for k in far:
            dest = lax.rem(o + k, NZ)
            send(buf.at[dest], slots.at[k - 1], s0 + k - 1, (t, dest))

    def scatter_z_sum(buf, slots, s0):
        total = buf[o].astype(F32)
        for k in range(1, NZ):
            arrived(slots.at[k - 1], s0 + k - 1)
            total = total + slots[k - 1].astype(F32)
        return total

    s_z = sem_ids(NZ - 1)
    s_b = sem_ids(NZ - 1)
    scatter_z(bdot(right[0], up_w, NT_DIMS), zs, zr, s_z)
    arrived(left_in, s_l)
    arrived(right_in, s_l + 1)
    both = bdot(left[c], right[c], TN_DIMS) + bdot(left_in[...], right_in[...], TN_DIMS)
    both = both.reshape(NY, NX, RB, HID)
    gf[...] = both
    gb[...] = both.astype(BF16)

    s_rx = sem_ids(3 * NY)
    s_ry = sem_ids(NY - 1)
    for k in far + (0,):
        row = lax.rem(y + k, NY)
        for n in range(1, NX):
            col = lax.rem(x + n, NX)
            send(gb.at[row, col], rx.at[row, n - 1], s_rx + 3 * k + n - 1, (tile_at(y, col), o))
    scatter_z(bdot(right[1], down_w, NT_DIMS), bs, br, s_b)
    total = None
    for k in far + (0,):
        row = lax.rem(y + k, NY)
        total = gf[row, x]
        for n in range(1, NX):
            arrived(rx.at[row, n - 1], s_rx + 3 * k + n - 1)
            total = total + rx[row, n - 1].astype(F32)
        if k:
            ty[row] = total.astype(BF16)
            send(ty.at[row], ry.at[k - 1], s_ry + k - 1, (tile_at(row, x), o))
    for k in near:
        arrived(ry.at[k - 1], s_ry + k - 1)
        total = total + ry[k - 1].astype(F32)
    grow[...] = total
    ga[y, x] = total.astype(BF16)
    s_gy = sem_ids(NY - 1)
    s_gx = sem_ids(3 * NY)
    gather_start(grad_at, s_gy, s_gx)

    gather_relay(grad_at, s_gy, s_gx, near[:4])

    grad_normed = scatter_z_sum(zs, zr, s_z)
    own_rows = pl.ds(pl.multiple_of(o * OWN_TOK, OWN_TOK), OWN_TOK)
    own_live = length > o // 2
    centred = mixed[own_rows, :]
    g = grad_normed * gain
    mean1 = jnp.sum(g, axis=-1, keepdims=True) * (1.0 / D)
    mean2 = jnp.sum(g * centred, axis=-1, keepdims=True) * (1.0 / D)
    grad_mixed = inv_s[own_rows, :] * (g - mean1 - centred * mean2)
    grad_mixed = jnp.where(own_live, grad_mixed, 0.0)
    hg[...] = grad_mixed.astype(BF16)
    s_h = sem_ids(2)
    s_ct = sem_ids(4)
    s_ch = sem_ids(1)
    send(hg, nb.at[0], s_h, (t, lax.rem(o + 1, NZ)))
    send(hg, nb.at[1], s_h + 1, (t, lax.rem(o + NZ - 1, NZ)))
    s_c4 = sem_ids(4)

    @pl.when(first_own)
    def _():
        for q in range(4):
            pltpu.make_async_remote_copy(
                src_ref=hg, dst_ref=chd, send_sem=ss.at[s_c4 + q], recv_sem=rs.at[s_ch],
                device_id=(dn_t, 2 * q + 1), device_id_type=MESH,
            ).start()

    @pl.when(odd_own)
    def _():
        q = o // 2
        pltpu.make_async_remote_copy(
            src_ref=hg, dst_ref=ct.at[q], send_sem=ss.at[s_c4], recv_sem=rs.at[s_ct + q],
            device_id=(up_t, 0), device_id_type=MESH,
        ).start()

    frame2[...] = jnp.zeros_like(frame2)
    for ch in range(CH):
        frame2[ch, 3:7, 3:11, :] = grad_mixed[:, 128 * ch : 128 * ch + 128].reshape(4, 8, 128)

    gather_relay(grad_at, s_gy, s_gx, near[4:])

    def gram_of(ks):
        for n, k in enumerate(ks):
            row = gather_row(grad_at, s_gx, k)
            gm16[n] = ga[row].astype(F32).reshape(96, HID).astype(BF16)
        g16 = gm16[0 : len(ks)].reshape(96 * len(ks), HID)
        return bdot(g16, g16, TN_DIMS)

    gram = gram_of((0,) + near[:4]) + gram_of(near[4:])
    eye = (
        lax.broadcasted_iota(jnp.int32, (HID, HID), 0) == lax.broadcasted_iota(jnp.int32, (HID, HID), 1)
    ).astype(F32)

    norm2 = jnp.sum(jnp.sum(gram * eye, axis=0, keepdims=True), axis=1, keepdims=True)
    root = lax.rsqrt(norm2 + EPS_NORM)
    gram = gram * (root * root)

    def times(a, b):
        return bdot(a.astype(BF16), b)

    def residue(a):
        a16 = a.astype(BF16)
        return (NS_B * a + NS_C * bdot(a16, a16)).astype(BF16)

    q0 = residue(gram)
    first = NS_A * gram + times(gram, q0)
    q1 = residue(NS_A * first + times(first, q0))
    ortho = grow[...] * root
    ortho = NS_A * ortho + times(ortho, q0)
    xo[c] = NS_A * ortho + times(ortho, q1)
    s_x = sem_ids(1)
    send(xo.at[c], xo.at[c], s_x, (sib, o))
    def put_before(block):
        rows3 = block.astype(F32)[8:32]
        for ch in range(CH):
            frame2[ch, 0:3, 3:11, :] = rows3[:, 128 * ch : 128 * ch + 128].reshape(3, 8, 128)

    def put_after(block):
        rows3 = block.astype(F32)[0:24]
        for ch in range(CH):
            frame2[ch, 7:10, 3:11, :] = rows3[:, 128 * ch : 128 * ch + 128].reshape(3, 8, 128)

    arrived(nb.at[0], s_h)
    arrived(nb.at[1], s_h + 1)

    @pl.when(first_own)
    def _():
        for q in range(4):
            arrived(ct.at[q], s_ct + q)
        prev_len = lens[dn_t]
        block = ct[0].astype(F32)
        for q in range(1, 4):
            block = jnp.where(prev_len == q + 1, ct[q].astype(F32), block)
        put_before(jnp.where(t > 0, block, 0.0))
        for q in range(4):
            pltpu.make_async_remote_copy(
                src_ref=hg, dst_ref=chd, send_sem=ss.at[s_c4 + q], recv_sem=rs.at[s_ch],
                device_id=(dn_t, 2 * q + 1), device_id_type=MESH,
            ).wait_send()

    @pl.when(jnp.logical_not(first_own))
    def _():
        put_before(nb[0])

    @pl.when(odd_own)
    def _():
        arrived(chd, s_ch)
        q = o // 2
        edge = jnp.where(t < NT - 1, chd[...].astype(F32), 0.0)
        put_after(jnp.where(length == q + 1, edge, nb[1].astype(F32)))
        pltpu.make_async_remote_copy(
            src_ref=hg, dst_ref=ct.at[q], send_sem=ss.at[s_c4], recv_sem=rs.at[s_ct + q],
            device_id=(up_t, 0), device_id_type=MESH,
        ).wait_send()

    @pl.when(jnp.logical_not(odd_own))
    def _():
        put_after(nb[1])

    def chunk2(ch, _):
        lanes = pl.ds(pl.multiple_of(ch * 128, 128), 128)
        acc = jnp.zeros((4, 8, 128), F32)
        for i in range(7):
            for j in range(7):
                w = dk[6 - i, 6 - j : 7 - j, lanes].reshape(1, 1, 128)
                acc = acc + w * frame2[ch, i : i + 4, j : j + 8, :]
        res = cot[own_rows, lanes].astype(F32) + acc.reshape(OWN_TOK, 128)
        tok_ref[1, :, lanes] = jnp.where(own_live, res, 0.0).astype(BF16)
        return 0

    lax.fori_loop(0, CH, chunk2, 0)

    branch = scatter_z_sum(bs, br, s_b)
    own_keep = jnp.where(own_live, tissue[o // 2], 0).astype(F32)
    res = feat[own_rows, :].astype(F32) + (own_keep * scale) * branch
    tok_ref[0] = jnp.where(own_live, res, 0.0).astype(BF16)

    arrived(xo.at[1 - c], s_x)
    for m in range(2):
        muon_ref[m] = jnp.where(c == 0, xo[m, 0:12, :], xo[m, 12:24, :])

    for cp in sent:
        cp.wait_send()


SEMS = 160


def shards(features, cotangent, depth_kernel, ln_gain, weight_up, bias_up, weight_down, layer_scale, tissue, lengths):
    vmem = pl.BlockSpec(memory_space=pltpu.VMEM)
    hbm = pl.BlockSpec(memory_space=pltpu.HBM)
    block4 = (NY, NX, RB, HID)
    scratch = [
        pltpu.SMEM((NT,), jnp.int32),
        pltpu.SMEM((4,), jnp.int32),
        pltpu.VMEM((TOK, D), BF16),
        pltpu.VMEM((TOK, D), BF16),
        pltpu.VMEM((7, 7, D), F32),
        pltpu.VMEM((D,), F32),
        pltpu.VMEM((HID,), F32),
        pltpu.VMEM((D,), F32),
        pltpu.VMEM((2, 12, HID), BF16),
        pltpu.VMEM((12, HID), BF16),
        pltpu.VMEM((24, HID), F32),
        pltpu.VMEM((2,) + block4, BF16),
        pltpu.VMEM((2, NY, 96, HID), BF16),
        pltpu.VMEM((2, 24, D), BF16),
        pltpu.VMEM((2, 24, D), BF16),
        pltpu.VMEM((CH, 38, 16, 128), F32),
        pltpu.VMEM((TOK, D), F32),
        pltpu.VMEM((TOK, 1), F32),
        pltpu.VMEM((2, TOK, D), BF16),
        pltpu.VMEM((2, TOK, HID), BF16),
        pltpu.VMEM((NZ, OWN_TOK, D), BF16),
        pltpu.VMEM((NZ - 1, OWN_TOK, D), BF16),
        pltpu.VMEM((NZ, OWN_TOK, D), BF16),
        pltpu.VMEM((NZ - 1, OWN_TOK, D), BF16),
        pltpu.VMEM((TOK, D), BF16),
        pltpu.VMEM((TOK, HID), BF16),
        pltpu.VMEM(block4, F32),
        pltpu.VMEM(block4, BF16),
        pltpu.VMEM((NY, NX - 1, RB, HID), BF16),
        pltpu.VMEM((NY, RB, HID), BF16),
        pltpu.VMEM((NY - 1, RB, HID), BF16),
        pltpu.VMEM((RB, HID), F32),
        pltpu.VMEM(block4, BF16),
        pltpu.VMEM((NY, 96, HID), BF16),
        pltpu.VMEM((OWN_TOK, D), BF16),
        pltpu.VMEM((2, OWN_TOK, D), BF16),
        pltpu.VMEM((4, OWN_TOK, D), BF16),
        pltpu.VMEM((OWN_TOK, D), BF16),
        pltpu.VMEM((CH, 10, 16, 128), F32),
        pltpu.VMEM((2, RB, HID), F32),
        pltpu.SemaphoreType.DMA((SEMS,)),
        pltpu.SemaphoreType.DMA((SEMS,)),
        pltpu.SemaphoreType.DMA((10,)),
    ]
    outs = pl.pallas_call(
        body,
        out_shape=(
            jax.ShapeDtypeStruct((2, OWN_TOK, D), BF16),
            jax.ShapeDtypeStruct((2, 12, HID), F32),
        ),
        in_specs=[hbm] * 10,
        out_specs=(vmem,) * 2,
        scratch_shapes=scratch,
        compiler_params=pltpu.CompilerParams(
            collective_id=0, has_side_effects=True, vmem_limit_bytes=62 << 20
        ),
    )(
        lengths,
        tissue.reshape(4),
        features.reshape(TOK, D),
        cotangent.reshape(TOK, D),
        depth_kernel,
        ln_gain,
        weight_up,
        bias_up,
        weight_down.T,
        layer_scale,
    )
    tokens, muon = outs
    return (
        tokens[0].reshape(4, 8, D),
        tokens[1].reshape(4, 8, D),
        muon[0],
        muon[1].T,
    )


def solution(mesh):
    in_specs = (
        P("tile", None, None),
        P("tile", None, None),
        P(),
        P(),
        P("tile", "own"),
        P("own"),
        P("own", "tile"),
        P(),
        P("tile", None),
        P(),
    )
    out_specs = (
        P(("tile", "own"), None, None),
        P(("tile", "own"), None, None),
        P("tile", "own"),
        P("own", "tile"),
    )
    return jax.shard_map(shards, mesh=mesh, in_specs=in_specs, out_specs=out_specs, check_vma=False)
```

```python
import jax
import jax.numpy as jnp
from jax import lax
from jax.experimental import pallas as pl
from jax.experimental.pallas import tpu as pltpu
from jax.sharding import PartitionSpec as P

MESH = pl.DeviceIdType.MESH
F32 = jnp.float32
BF16 = jnp.bfloat16

NY, NX, NZ = 8, 4, 8
NT = NY * NX * 2
D = 768
HID = 384
TOK = 256
CH = D // 128
RB = 24
OWN_TOK = 32

INV_ROOT_TWO = 0.7071067811865476
INV_ROOT_TAU = 0.3989422804014327
NS_A = 3.4445
NS_B = -4.775
NS_C = 2.0315
EPS_NORM = 1e-06


def bdot(a, b, dims=(((1,), (0,)), ((), ()))):
    return lax.dot_general(a, b, dims, preferred_element_type=F32)


NT_DIMS = (((1,), (1,)), ((), ()))
TN_DIMS = (((0,), (0,)), ((), ()))


def body(
    lens_h, tissue_h, feat_h, cot_h, dk_h, gain_h, wu_h, bias_h, wd_h, scale_h,
    tok_ref, muon_ref,
    lens, tissue, feat, cot, dk, gain1, bias1, scale1, pieces, piece_in, t24, wg, wm, rim, halo, frame, mixed, inv_s, left, right,
    zs, zr, bs, br, left_in, right_in, gf, gb, rx, ty, ry, grow, ga, gm16, hg, nb, ct, chd, frame2, xo,
    ss, rs, ls,
):
    t = lax.axis_index("tile")
    o = lax.axis_index("own")
    c = lax.rem(t, 2)
    chip = t // 2
    x = lax.rem(chip, NX)
    y = chip // NX
    sib = t + 1 - 2 * c

    def tile_at(yy, xx):
        return (yy * NX + xx) * 2 + c

    counter = [0]
    sent = []
    along_z = []

    def sem_ids(n):
        first = counter[0]
        counter[0] += n
        return first

    def copy(src, dst, sem, dev):
        return pltpu.make_async_remote_copy(
            src_ref=src, dst_ref=dst, send_sem=ss.at[sem], recv_sem=rs.at[sem],
            device_id=dev, device_id_type=MESH,
        )

    def send(src, dst, sem, dev):
        cp = copy(src, dst, sem, dev)
        cp.start()
        sent.append(cp)

    def drain():
        for cp in sent:
            cp.wait_send()
        sent.clear()

    def arrived(dst, sem):
        copy(dst, dst, sem, (t, o)).wait_recv()

    fetches = {}
    for n, (name, src, dst) in enumerate(
        (
            ("wu", wu_h, pieces.at[0]), ("wd", wd_h, pieces.at[1]), ("lens", lens_h, lens),
            ("feat", feat_h, feat), ("tissue", tissue_h, tissue), ("dk", dk_h, dk), ("gain", gain_h, gain1),
            ("scale", scale_h, scale1), ("cot", cot_h, cot), ("bias", bias_h, bias1),
        )
    ):
        fetches[name] = pltpu.make_async_copy(src, dst, ls.at[n])
        fetches[name].start()

    bar = pltpu.get_barrier_semaphore()

    def greet(dev):
        pl.semaphore_signal(bar, inc=1, device_id=dev, device_id_type=MESH)

    up_t = lax.rem(t + 1, NT)
    dn_t = lax.rem(t + NT - 1, NT)
    greet((sib, o))
    for k in range(1, NY):
        greet((tile_at(lax.rem(y + k, NY), x), o))
    for k in range(1, NX):
        greet((tile_at(y, lax.rem(x + k, NX)), o))
    for k in range(1, NZ):
        greet((t, lax.rem(o + k, NZ)))
    greet((up_t, o))
    greet((dn_t, o))
    first_own = o == 0
    odd_own = lax.rem(o, 2) == 1

    @pl.when(first_own)
    def _():
        for q in range(4):
            greet((dn_t, 2 * q + 1))

    @pl.when(odd_own)
    def _():
        greet((up_t, 0))

    expected = 1 + (NY - 1) + (NX - 1) + (NZ - 1) + 2
    fetches["wu"].wait()
    fetches["wd"].wait()
    pl.semaphore_wait(bar, expected + 4 * ((NZ - o) // NZ) + lax.rem(o, 2))

    s_piece = sem_ids(1)
    send(pieces.at[1 - c], piece_in, s_piece, (sib, o))

    near = (1, 7, 2, 6, 3, 5, 4)
    far = near[::-1]

    def row_of(k):
        return lax.rem(y + NY - k, NY)

    def share_x(at, row, sem):
        for k in range(1, NX):
            send(at(row, x), at(row, x), sem + k - 1, (tile_at(y, lax.rem(x + k, NX)), o))

    def gather_start(at, s_y, s_x):
        for k in near:
            send(at(y, x), at(y, x), s_y + k - 1, (tile_at(lax.rem(y + k, NY), x), o))
        share_x(at, y, s_x)

    def gather_relay(at, s_y, s_x, ks):
        for k in ks:
            row = row_of(k)
            arrived(at(row, x), s_y + k - 1)
            share_x(at, row, s_x + 3 * k)

    def gather_row(at, s_x, k):
        row = row_of(k)
        for n in range(1, NX):
            arrived(at(row, lax.rem(x + NX - n, NX)), s_x + 3 * k + n - 1)
        return row

    def weight_at(row, col):
        return wg.at[c, row, col]

    def grad_at(row, col):
        return ga.at[row, col]

    s_wy = sem_ids(NY - 1)
    s_wx = sem_ids(3 * NY)
    s_ws = sem_ids(NY)
    fetches["lens"].wait()
    fetches["feat"].wait()
    length = lens[t]
    rim[0] = feat[0:24, :].astype(F32).astype(BF16)
    tail = feat[0:64, :].astype(F32)[40:64]
    for q in range(1, 4):
        tail = jnp.where(length == q + 1, feat[64 * q : 64 * q + 64, :].astype(F32)[40:64], tail)
    rim[1] = tail.astype(BF16)
    s_halo = sem_ids(2)
    send(rim.at[1], halo.at[0], s_halo, (up_t, o))
    send(rim.at[0], halo.at[1], s_halo + 1, (dn_t, o))

    arrived(piece_in, s_piece)
    mine = pieces[c].astype(F32)
    other = piece_in[...].astype(F32)
    t24[0:12, :] = jnp.where(c == 0, mine, other)
    t24[12:24, :] = jnp.where(c == 0, other, mine)
    wg[c, y, x] = t24[...].astype(BF16)
    gather_start(weight_at, s_wy, s_wx)

    for name in ("tissue", "dk", "gain", "scale", "cot", "bias"):
        fetches[name].wait()
    gain = gain1[...].reshape(1, D)
    scale = scale1[...].reshape(1, D)
    frame[...] = jnp.zeros_like(frame)
    for q in range(4):
        rows = slice(64 * q, 64 * q + 64)
        live = length > q
        keep = jnp.where(live, tissue[q], 0).astype(F32)
        f = feat[rows, :].astype(F32)
        if q:
            f = jnp.where(live, f, 0.0)
        for ch in range(CH):
            frame[ch, 3 + 8 * q : 11 + 8 * q, 3:11, :] = f[:, 128 * ch : 128 * ch + 128].reshape(8, 8, 128)
        left[1, rows, :] = ((keep * scale) * cot[rows, :].astype(F32)).astype(BF16)

    arrived(halo.at[0], s_halo)
    arrived(halo.at[1], s_halo + 1)
    before = jnp.where(t > 0, halo[0].astype(F32), 0.0)
    after = jnp.where(t < NT - 1, halo[1].astype(F32), 0.0)
    for ch in range(CH):
        lanes = slice(128 * ch, 128 * ch + 128)
        frame[ch, 0:3, 3:11, :] = before[:, lanes].reshape(3, 8, 128)
        nxt = after[:, lanes].reshape(3, 8, 128)
        for q in range(1, 4):
            old = frame[ch, 3 + 8 * q : 6 + 8 * q, 3:11, :]
            frame[ch, 3 + 8 * q : 6 + 8 * q, 3:11, :] = jnp.where(length == q, nxt, old)
        frame[ch, 35:38, 3:11, :] = jnp.where(length == 4, nxt, 0.0)

    def conv_half(h):
        def chunk(ch, _):
            lanes = pl.ds(pl.multiple_of(ch * 128, 128), 128)
            acc = jnp.zeros((16, 8, 128), F32)
            for i in range(7):
                for j in range(7):
                    w = dk[i, j : j + 1, lanes].reshape(1, 1, 128)
                    acc = acc + w * frame[ch, 16 * h + i : 16 * h + i + 16, j : j + 8, :]
            mixed[128 * h : 128 * h + 128, lanes] = acc.reshape(128, 128)
            return 0

        lax.fori_loop(0, CH, chunk, 0)

    gather_relay(weight_at, s_wy, s_wx, near[:2])
    conv_half(0)
    gather_relay(weight_at, s_wy, s_wx, near[2:6])
    conv_half(1)

    for q in range(4):
        rows = slice(64 * q, 64 * q + 64)
        m = mixed[rows, :]
        shifted = m - jnp.sum(m, axis=-1, keepdims=True) * (1.0 / D)
        var = jnp.sum(shifted * shifted, axis=-1, keepdims=True) * (1.0 / D)
        inv = lax.rsqrt(var + 1e-06)
        centred = shifted * inv
        mixed[rows, :] = centred
        inv_s[rows, :] = inv
        left[0, rows, :] = (centred * gain).astype(BF16)

    gather_relay(weight_at, s_wy, s_wx, near[6:])
    s_l = sem_ids(2)
    send(left.at[1 - c], left_in, s_l, (sib, o))

    def take(m, k):
        wm[m, row_of(k)] = wg[m, row_of(k)].astype(F32).reshape(96, HID).astype(BF16)

    def take_other(k):
        arrived(wg.at[1 - c, row_of(k)], s_ws + k)
        take(1 - c, k)

    last = None
    for k in (0,) + near:
        row = gather_row(weight_at, s_wx, k)
        send(wg.at[c, row], wg.at[c, row], s_ws + k, (sib, o))
        take(c, k)
        if last is not None:
            take_other(last)
        last = k
    take_other(last)

    up_w = wm[0].reshape(D, HID)
    down_w = wm[1].reshape(D, HID)
    hidden = bdot(left[0], up_w) + bias1[...].reshape(1, HID)
    phi = 0.5 * (1.0 + lax.erf(hidden * INV_ROOT_TWO))
    right[1] = (hidden * phi).astype(BF16)
    grad_act = bdot(left[1], down_w)
    slope = phi + hidden * jnp.exp(-0.5 * hidden * hidden) * INV_ROOT_TAU
    right[0] = (grad_act * slope).astype(BF16)

    send(right.at[1 - c], right_in, s_l + 1, (sib, o))

    def scatter_z(value, buf, slots, s0):
        buf[...] = value.reshape(NZ, OWN_TOK, D).astype(BF16)
        for k in far:
            dest = lax.rem(o + k, NZ)
            cp = copy(buf.at[dest], slots.at[k - 1], s0 + k - 1, (t, dest))
            cp.start()
            along_z.append(cp)

    def scatter_z_sum(buf, slots, s0):
        total = buf[o].astype(F32)
        for k in range(1, NZ):
            arrived(slots.at[k - 1], s0 + k - 1)
            total = total + slots[k - 1].astype(F32)
        return total

    s_z = sem_ids(NZ - 1)
    s_b = sem_ids(NZ - 1)
    scatter_z(bdot(right[0], up_w, NT_DIMS), zs, zr, s_z)
    arrived(left_in, s_l)
    arrived(right_in, s_l + 1)
    both = bdot(left[c], right[c], TN_DIMS) + bdot(left_in[...], right_in[...], TN_DIMS)
    both = both.reshape(NY, NX, RB, HID)
    gf[...] = both
    gb[...] = both.astype(BF16)

    early = list(sent)
    sent.clear()

    s_rx = sem_ids(3 * NY)
    s_ry = sem_ids(NY - 1)
    for k in far + (0,):
        row = lax.rem(y + k, NY)
        for n in range(1, NX):
            col = lax.rem(x + n, NX)
            send(gb.at[row, col], rx.at[row, n - 1], s_rx + 3 * k + n - 1, (tile_at(y, col), o))
    scatter_z(bdot(right[1], down_w, NT_DIMS), bs, br, s_b)
    for cp in early:
        cp.wait_send()
    total = None
    for k in far + (0,):
        row = lax.rem(y + k, NY)
        total = gf[row, x]
        for n in range(1, NX):
            arrived(rx.at[row, n - 1], s_rx + 3 * k + n - 1)
            total = total + rx[row, n - 1].astype(F32)
        if k:
            ty[row] = total.astype(BF16)
            send(ty.at[row], ry.at[k - 1], s_ry + k - 1, (tile_at(row, x), o))
    for k in near:
        arrived(ry.at[k - 1], s_ry + k - 1)
        total = total + ry[k - 1].astype(F32)
    grow[...] = total
    ga[y, x] = total.astype(BF16)
    s_gy = sem_ids(NY - 1)
    s_gx = sem_ids(3 * NY)
    early = list(sent)
    sent.clear()
    gather_start(grad_at, s_gy, s_gx)
    for cp in early:
        cp.wait_send()

    gather_relay(grad_at, s_gy, s_gx, near[:4])

    grad_normed = scatter_z_sum(zs, zr, s_z)
    own_rows = pl.ds(pl.multiple_of(o * OWN_TOK, OWN_TOK), OWN_TOK)
    own_live = length > o // 2
    centred = mixed[own_rows, :]
    g = grad_normed * gain
    mean1 = jnp.sum(g, axis=-1, keepdims=True) * (1.0 / D)
    mean2 = jnp.sum(g * centred, axis=-1, keepdims=True) * (1.0 / D)
    grad_mixed = inv_s[own_rows, :] * (g - mean1 - centred * mean2)
    grad_mixed = jnp.where(own_live, grad_mixed, 0.0)
    hg[...] = grad_mixed.astype(BF16)
    s_h = sem_ids(2)
    s_ct = sem_ids(4)
    s_ch = sem_ids(1)
    send(hg, nb.at[0], s_h, (t, lax.rem(o + 1, NZ)))
    send(hg, nb.at[1], s_h + 1, (t, lax.rem(o + NZ - 1, NZ)))
    s_c4 = sem_ids(4)

    @pl.when(first_own)
    def _():
        for q in range(4):
            pltpu.make_async_remote_copy(
                src_ref=hg, dst_ref=chd, send_sem=ss.at[s_c4 + q], recv_sem=rs.at[s_ch],
                device_id=(dn_t, 2 * q + 1), device_id_type=MESH,
            ).start()

    @pl.when(odd_own)
    def _():
        q = o // 2
        pltpu.make_async_remote_copy(
            src_ref=hg, dst_ref=ct.at[q], send_sem=ss.at[s_c4], recv_sem=rs.at[s_ct + q],
            device_id=(up_t, 0), device_id_type=MESH,
        ).start()

    frame2[...] = jnp.zeros_like(frame2)
    for ch in range(CH):
        frame2[ch, 3:7, 3:11, :] = grad_mixed[:, 128 * ch : 128 * ch + 128].reshape(4, 8, 128)

    gather_relay(grad_at, s_gy, s_gx, near[4:])

    def gram_of(ks):
        for n, k in enumerate(ks):
            row = gather_row(grad_at, s_gx, k)
            gm16[n] = ga[row].astype(F32).reshape(96, HID).astype(BF16)
        g16 = gm16[0 : len(ks)].reshape(96 * len(ks), HID)
        return bdot(g16, g16, TN_DIMS)

    drain()
    gram = gram_of((0,) + near[:4])

    def put_before(block):
        rows3 = block.astype(F32)[8:32]
        for ch in range(CH):
            frame2[ch, 0:3, 3:11, :] = rows3[:, 128 * ch : 128 * ch + 128].reshape(3, 8, 128)

    def put_after(block):
        rows3 = block.astype(F32)[0:24]
        for ch in range(CH):
            frame2[ch, 7:10, 3:11, :] = rows3[:, 128 * ch : 128 * ch + 128].reshape(3, 8, 128)

    arrived(nb.at[0], s_h)
    arrived(nb.at[1], s_h + 1)

    @pl.when(first_own)
    def _():
        for q in range(4):
            arrived(ct.at[q], s_ct + q)
        prev_len = lens[dn_t]
        block = ct[0].astype(F32)
        for q in range(1, 4):
            block = jnp.where(prev_len == q + 1, ct[q].astype(F32), block)
        put_before(jnp.where(t > 0, block, 0.0))
        for q in range(4):
            pltpu.make_async_remote_copy(
                src_ref=hg, dst_ref=chd, send_sem=ss.at[s_c4 + q], recv_sem=rs.at[s_ch],
                device_id=(dn_t, 2 * q + 1), device_id_type=MESH,
            ).wait_send()

    @pl.when(jnp.logical_not(first_own))
    def _():
        put_before(nb[0])

    @pl.when(odd_own)
    def _():
        arrived(chd, s_ch)
        q = o // 2
        edge = jnp.where(t < NT - 1, chd[...].astype(F32), 0.0)
        put_after(jnp.where(length == q + 1, edge, nb[1].astype(F32)))
        pltpu.make_async_remote_copy(
            src_ref=hg, dst_ref=ct.at[q], send_sem=ss.at[s_c4], recv_sem=rs.at[s_ct + q],
            device_id=(up_t, 0), device_id_type=MESH,
        ).wait_send()

    @pl.when(jnp.logical_not(odd_own))
    def _():
        put_after(nb[1])

    def chunk2(ch, _):
        lanes = pl.ds(pl.multiple_of(ch * 128, 128), 128)
        acc = jnp.zeros((4, 8, 128), F32)
        for i in range(7):
            for j in range(7):
                w = dk[6 - i, 6 - j : 7 - j, lanes].reshape(1, 1, 128)
                acc = acc + w * frame2[ch, i : i + 4, j : j + 8, :]
        res = cot[own_rows, lanes].astype(F32) + acc.reshape(OWN_TOK, 128)
        tok_ref[1, :, lanes] = jnp.where(own_live, res, 0.0).astype(BF16)
        return 0

    lax.fori_loop(0, CH, chunk2, 0)

    gram = gram + gram_of(near[4:])
    eye = (
        lax.broadcasted_iota(jnp.int32, (HID, HID), 0) == lax.broadcasted_iota(jnp.int32, (HID, HID), 1)
    ).astype(F32)

    norm2 = jnp.sum(jnp.sum(gram * eye, axis=0, keepdims=True), axis=1, keepdims=True)
    root = lax.rsqrt(norm2 + EPS_NORM)
    gram = gram * (root * root)

    def times(a, b):
        return bdot(a.astype(BF16), b)

    def residue(a):
        a16 = a.astype(BF16)
        return (NS_B * a + NS_C * bdot(a16, a16)).astype(BF16)

    q0 = residue(gram)
    first = NS_A * gram + times(gram, q0)
    q1 = residue(NS_A * first + times(first, q0))
    ortho = grow[...] * root
    ortho = NS_A * ortho + times(ortho, q0)
    xo[c] = NS_A * ortho + times(ortho, q1)
    s_x = sem_ids(1)
    send(xo.at[c], xo.at[c], s_x, (sib, o))
    branch = scatter_z_sum(bs, br, s_b)
    own_keep = jnp.where(own_live, tissue[o // 2], 0).astype(F32)
    res = feat[own_rows, :].astype(F32) + (own_keep * scale) * branch
    tok_ref[0] = jnp.where(own_live, res, 0.0).astype(BF16)

    arrived(xo.at[1 - c], s_x)
    for m in range(2):
        muon_ref[m] = jnp.where(c == 0, xo[m, 0:12, :], xo[m, 12:24, :])

    for cp in sent + along_z:
        cp.wait_send()


SEMS = 160


def shards(features, cotangent, depth_kernel, ln_gain, weight_up, bias_up, weight_down, layer_scale, tissue, lengths):
    vmem = pl.BlockSpec(memory_space=pltpu.VMEM)
    hbm = pl.BlockSpec(memory_space=pltpu.HBM)
    block4 = (NY, NX, RB, HID)
    scratch = [
        pltpu.SMEM((NT,), jnp.int32),
        pltpu.SMEM((4,), jnp.int32),
        pltpu.VMEM((TOK, D), BF16),
        pltpu.VMEM((TOK, D), BF16),
        pltpu.VMEM((7, 7, D), F32),
        pltpu.VMEM((D,), F32),
        pltpu.VMEM((HID,), F32),
        pltpu.VMEM((D,), F32),
        pltpu.VMEM((2, 12, HID), BF16),
        pltpu.VMEM((12, HID), BF16),
        pltpu.VMEM((24, HID), F32),
        pltpu.VMEM((2,) + block4, BF16),
        pltpu.VMEM((2, NY, 96, HID), BF16),
        pltpu.VMEM((2, 24, D), BF16),
        pltpu.VMEM((2, 24, D), BF16),
        pltpu.VMEM((CH, 38, 16, 128), F32),
        pltpu.VMEM((TOK, D), F32),
        pltpu.VMEM((TOK, 1), F32),
        pltpu.VMEM((2, TOK, D), BF16),
        pltpu.VMEM((2, TOK, HID), BF16),
        pltpu.VMEM((NZ, OWN_TOK, D), BF16),
        pltpu.VMEM((NZ - 1, OWN_TOK, D), BF16),
        pltpu.VMEM((NZ, OWN_TOK, D), BF16),
        pltpu.VMEM((NZ - 1, OWN_TOK, D), BF16),
        pltpu.VMEM((TOK, D), BF16),
        pltpu.VMEM((TOK, HID), BF16),
        pltpu.VMEM(block4, F32),
        pltpu.VMEM(block4, BF16),
        pltpu.VMEM((NY, NX - 1, RB, HID), BF16),
        pltpu.VMEM((NY, RB, HID), BF16),
        pltpu.VMEM((NY - 1, RB, HID), BF16),
        pltpu.VMEM((RB, HID), F32),
        pltpu.VMEM(block4, BF16),
        pltpu.VMEM((NY, 96, HID), BF16),
        pltpu.VMEM((OWN_TOK, D), BF16),
        pltpu.VMEM((2, OWN_TOK, D), BF16),
        pltpu.VMEM((4, OWN_TOK, D), BF16),
        pltpu.VMEM((OWN_TOK, D), BF16),
        pltpu.VMEM((CH, 10, 16, 128), F32),
        pltpu.VMEM((2, RB, HID), F32),
        pltpu.SemaphoreType.DMA((SEMS,)),
        pltpu.SemaphoreType.DMA((SEMS,)),
        pltpu.SemaphoreType.DMA((10,)),
    ]
    outs = pl.pallas_call(
        body,
        out_shape=(
            jax.ShapeDtypeStruct((2, OWN_TOK, D), BF16),
            jax.ShapeDtypeStruct((2, 12, HID), F32),
        ),
        in_specs=[hbm] * 10,
        out_specs=(vmem,) * 2,
        scratch_shapes=scratch,
        compiler_params=pltpu.CompilerParams(
            collective_id=0, has_side_effects=True, vmem_limit_bytes=62 << 20
        ),
    )(
        lengths,
        tissue.reshape(4),
        features.reshape(TOK, D),
        cotangent.reshape(TOK, D),
        depth_kernel,
        ln_gain,
        weight_up,
        bias_up,
        weight_down.T,
        layer_scale,
    )
    tokens, muon = outs
    return (
        tokens[0].reshape(4, 8, D),
        tokens[1].reshape(4, 8, D),
        muon[0],
        muon[1].T,
    )


def solution(mesh):
    in_specs = (
        P("tile", None, None),
        P("tile", None, None),
        P(),
        P(),
        P("tile", "own"),
        P("own"),
        P("own", "tile"),
        P(),
        P("tile", None),
        P(),
    )
    out_specs = (
        P(("tile", "own"), None, None),
        P(("tile", "own"), None, None),
        P("tile", "own"),
        P("own", "tile"),
    )
    return jax.shard_map(shards, mesh=mesh, in_specs=in_specs, out_specs=out_specs, check_vma=False)
```

```python
import jax
import jax.numpy as jnp
from jax import lax
from jax.experimental import pallas as pl
from jax.experimental.pallas import tpu as pltpu
from jax.sharding import PartitionSpec as P

MESH = pl.DeviceIdType.MESH
F32 = jnp.float32
BF16 = jnp.bfloat16

NY, NX, NZ = 8, 4, 8
NT = NY * NX * 2
D = 768
HID = 384
TOK = 256
CH = D // 128
RB = 24
OWN_TOK = 32

INV_ROOT_TWO = 0.7071067811865476
INV_ROOT_TAU = 0.3989422804014327
NS_A = 3.4445
NS_B = -4.775
NS_C = 2.0315
EPS_NORM = 1e-06


def bdot(a, b, dims=(((1,), (0,)), ((), ()))):
    return lax.dot_general(a, b, dims, preferred_element_type=F32)


NT_DIMS = (((1,), (1,)), ((), ()))
TN_DIMS = (((0,), (0,)), ((), ()))


def body(
    lens_h, tissue_h, feat_h, cot_h, dk_h, gain_h, wu_h, bias_h, wd_h, scale_h,
    tok_ref, muon_ref,
    lens, tissue, feat, cot, dk, gain1, bias1, scale1, pieces, piece_in, t24, wg, wm, rim, halo, frame, mixed, inv_s, left, right,
    zs, zr, bs, br, left_in, right_in, gf, gb, rx, ty, ry, grow, ga, gm16, hg, nb, ct, chd, frame2, xo,
    ss, rs, ls,
):
    t = lax.axis_index("tile")
    o = lax.axis_index("own")
    c = lax.rem(t, 2)
    chip = t // 2
    x = lax.rem(chip, NX)
    y = chip // NX
    sib = t + 1 - 2 * c

    def tile_at(yy, xx):
        return (yy * NX + xx) * 2 + c

    counter = [0]
    sent = []
    along_z = []

    def sem_ids(n):
        first = counter[0]
        counter[0] += n
        return first

    def copy(src, dst, sem, dev):
        return pltpu.make_async_remote_copy(
            src_ref=src, dst_ref=dst, send_sem=ss.at[sem], recv_sem=rs.at[sem],
            device_id=dev, device_id_type=MESH,
        )

    def send(src, dst, sem, dev):
        cp = copy(src, dst, sem, dev)
        cp.start()
        sent.append(cp)

    def drain():
        for cp in sent:
            cp.wait_send()
        sent.clear()

    def arrived(dst, sem):
        copy(dst, dst, sem, (t, o)).wait_recv()

    fetches = {}
    for n, (name, src, dst) in enumerate(
        (
            ("wu", wu_h, pieces.at[0]), ("wd", wd_h, pieces.at[1]), ("lens", lens_h, lens),
            ("feat", feat_h, feat), ("tissue", tissue_h, tissue), ("dk", dk_h, dk), ("gain", gain_h, gain1),
            ("scale", scale_h, scale1), ("cot", cot_h, cot), ("bias", bias_h, bias1),
        )
    ):
        fetches[name] = pltpu.make_async_copy(src, dst, ls.at[n])
        fetches[name].start()

    bar = pltpu.get_barrier_semaphore()

    def greet(dev):
        pl.semaphore_signal(bar, inc=1, device_id=dev, device_id_type=MESH)

    up_t = lax.rem(t + 1, NT)
    dn_t = lax.rem(t + NT - 1, NT)
    greet((sib, o))
    for k in range(1, NY):
        greet((tile_at(lax.rem(y + k, NY), x), o))
    for k in range(1, NX):
        greet((tile_at(y, lax.rem(x + k, NX)), o))
    for k in range(1, NZ):
        greet((t, lax.rem(o + k, NZ)))
    greet((up_t, o))
    greet((dn_t, o))
    first_own = o == 0
    odd_own = lax.rem(o, 2) == 1

    @pl.when(first_own)
    def _():
        for q in range(4):
            greet((dn_t, 2 * q + 1))

    @pl.when(odd_own)
    def _():
        greet((up_t, 0))

    expected = 1 + (NY - 1) + (NX - 1) + (NZ - 1) + 2
    fetches["wu"].wait()
    fetches["wd"].wait()
    pl.semaphore_wait(bar, expected + 4 * ((NZ - o) // NZ) + lax.rem(o, 2))

    s_piece = sem_ids(1)
    send(pieces.at[1 - c], piece_in, s_piece, (sib, o))

    near = (1, 7, 2, 6, 3, 5, 4)
    far = near[::-1]

    def row_of(k):
        return lax.rem(y + NY - k, NY)

    def share_x(at, row, sem):
        for k in range(1, NX):
            send(at(row, x), at(row, x), sem + k - 1, (tile_at(y, lax.rem(x + k, NX)), o))

    def gather_start(at, s_y, s_x):
        for k in near:
            send(at(y, x), at(y, x), s_y + k - 1, (tile_at(lax.rem(y + k, NY), x), o))
        share_x(at, y, s_x)

    def gather_relay(at, s_y, s_x, ks):
        for k in ks:
            row = row_of(k)
            arrived(at(row, x), s_y + k - 1)
            share_x(at, row, s_x + 3 * k)

    def gather_row(at, s_x, k):
        row = row_of(k)
        for n in range(1, NX):
            arrived(at(row, lax.rem(x + NX - n, NX)), s_x + 3 * k + n - 1)
        return row

    def weight_at(row, col):
        return wg.at[c, row, col]

    def grad_at(row, col):
        return ga.at[row, col]

    s_wy = sem_ids(NY - 1)
    s_wx = sem_ids(3 * NY)
    s_ws = sem_ids(NY)
    fetches["lens"].wait()
    fetches["feat"].wait()
    length = lens[t]
    rim[0] = feat[0:24, :].astype(F32).astype(BF16)
    tail = feat[0:64, :].astype(F32)[40:64]
    for q in range(1, 4):
        tail = jnp.where(length == q + 1, feat[64 * q : 64 * q + 64, :].astype(F32)[40:64], tail)
    rim[1] = tail.astype(BF16)
    s_halo = sem_ids(2)
    send(rim.at[1], halo.at[0], s_halo, (up_t, o))
    send(rim.at[0], halo.at[1], s_halo + 1, (dn_t, o))

    arrived(piece_in, s_piece)
    mine = pieces[c].astype(F32)
    other = piece_in[...].astype(F32)
    t24[0:12, :] = jnp.where(c == 0, mine, other)
    t24[12:24, :] = jnp.where(c == 0, other, mine)
    wg[c, y, x] = t24[...].astype(BF16)
    gather_start(weight_at, s_wy, s_wx)

    for name in ("tissue", "dk", "gain", "scale", "cot", "bias"):
        fetches[name].wait()
    gain = gain1[...].reshape(1, D)
    scale = scale1[...].reshape(1, D)
    frame[...] = jnp.zeros_like(frame)
    for q in range(4):
        rows = slice(64 * q, 64 * q + 64)
        live = length > q
        keep = jnp.where(live, tissue[q], 0).astype(F32)
        f = feat[rows, :].astype(F32)
        if q:
            f = jnp.where(live, f, 0.0)
        for ch in range(CH):
            frame[ch, 3 + 8 * q : 11 + 8 * q, 3:11, :] = f[:, 128 * ch : 128 * ch + 128].reshape(8, 8, 128)
        left[1, rows, :] = ((keep * scale) * cot[rows, :].astype(F32)).astype(BF16)

    gather_relay(weight_at, s_wy, s_wx, near[:2])

    arrived(halo.at[0], s_halo)
    arrived(halo.at[1], s_halo + 1)
    before = jnp.where(t > 0, halo[0].astype(F32), 0.0)
    after = jnp.where(t < NT - 1, halo[1].astype(F32), 0.0)
    for ch in range(CH):
        lanes = slice(128 * ch, 128 * ch + 128)
        frame[ch, 0:3, 3:11, :] = before[:, lanes].reshape(3, 8, 128)
        nxt = after[:, lanes].reshape(3, 8, 128)
        for q in range(1, 4):
            old = frame[ch, 3 + 8 * q : 6 + 8 * q, 3:11, :]
            frame[ch, 3 + 8 * q : 6 + 8 * q, 3:11, :] = jnp.where(length == q, nxt, old)
        frame[ch, 35:38, 3:11, :] = jnp.where(length == 4, nxt, 0.0)

    def conv_half(h):
        def chunk(ch, _):
            lanes = pl.ds(pl.multiple_of(ch * 128, 128), 128)
            acc = jnp.zeros((16, 8, 128), F32)
            for i in range(7):
                for j in range(7):
                    w = dk[i, j : j + 1, lanes].reshape(1, 1, 128)
                    acc = acc + w * frame[ch, 16 * h + i : 16 * h + i + 16, j : j + 8, :]
            mixed[128 * h : 128 * h + 128, lanes] = acc.reshape(128, 128)
            return 0

        lax.fori_loop(0, CH, chunk, 0)

    conv_half(0)
    gather_relay(weight_at, s_wy, s_wx, near[2:6])
    conv_half(1)

    for q in range(4):
        rows = slice(64 * q, 64 * q + 64)
        m = mixed[rows, :]
        shifted = m - jnp.sum(m, axis=-1, keepdims=True) * (1.0 / D)
        var = jnp.sum(shifted * shifted, axis=-1, keepdims=True) * (1.0 / D)
        inv = lax.rsqrt(var + 1e-06)
        centred = shifted * inv
        mixed[rows, :] = centred
        inv_s[rows, :] = inv
        left[0, rows, :] = (centred * gain).astype(BF16)

    gather_relay(weight_at, s_wy, s_wx, near[6:])
    s_l = sem_ids(2)
    send(left.at[1 - c], left_in, s_l, (sib, o))

    def take(m, k):
        wm[m, row_of(k)] = wg[m, row_of(k)].astype(F32).reshape(96, HID).astype(BF16)

    def take_other(k):
        arrived(wg.at[1 - c, row_of(k)], s_ws + k)
        take(1 - c, k)

    last = None
    for k in (0,) + near:
        row = gather_row(weight_at, s_wx, k)
        send(wg.at[c, row], wg.at[c, row], s_ws + k, (sib, o))
        take(c, k)
        if last is not None:
            take_other(last)
        last = k
    take_other(last)

    up_w = wm[0].reshape(D, HID)
    down_w = wm[1].reshape(D, HID)
    hidden = bdot(left[0], up_w) + bias1[...].reshape(1, HID)
    phi = 0.5 * (1.0 + lax.erf(hidden * INV_ROOT_TWO))
    right[1] = (hidden * phi).astype(BF16)
    grad_act = bdot(left[1], down_w)
    slope = phi + hidden * jnp.exp(-0.5 * hidden * hidden) * INV_ROOT_TAU
    right[0] = (grad_act * slope).astype(BF16)

    send(right.at[1 - c], right_in, s_l + 1, (sib, o))

    def scatter_z(value, buf, slots, s0):
        buf[...] = value.reshape(NZ, OWN_TOK, D).astype(BF16)
        for k in far:
            dest = lax.rem(o + k, NZ)
            cp = copy(buf.at[dest], slots.at[k - 1], s0 + k - 1, (t, dest))
            cp.start()
            along_z.append(cp)

    def scatter_z_sum(buf, slots, s0):
        total = buf[o].astype(F32)
        for k in range(1, NZ):
            arrived(slots.at[k - 1], s0 + k - 1)
            total = total + slots[k - 1].astype(F32)
        return total

    s_z = sem_ids(NZ - 1)
    s_b = sem_ids(NZ - 1)
    scatter_z(bdot(right[0], up_w, NT_DIMS), zs, zr, s_z)
    arrived(left_in, s_l)
    arrived(right_in, s_l + 1)
    both = bdot(left[c], right[c], TN_DIMS) + bdot(left_in[...], right_in[...], TN_DIMS)
    both = both.reshape(NY, NX, RB, HID)
    gf[...] = both
    gb[...] = both.astype(BF16)

    early = list(sent)
    sent.clear()

    s_rx = sem_ids(3 * NY)
    s_ry = sem_ids(NY - 1)
    for k in far + (0,):
        row = lax.rem(y + k, NY)
        for n in range(1, NX):
            col = lax.rem(x + n, NX)
            send(gb.at[row, col], rx.at[row, n - 1], s_rx + 3 * k + n - 1, (tile_at(y, col), o))
    scatter_z(bdot(right[1], down_w, NT_DIMS), bs, br, s_b)
    for cp in early:
        cp.wait_send()
    total = None
    for k in far + (0,):
        row = lax.rem(y + k, NY)
        total = gf[row, x]
        for n in range(1, NX):
            arrived(rx.at[row, n - 1], s_rx + 3 * k + n - 1)
            total = total + rx[row, n - 1].astype(F32)
        if k:
            ty[row] = total.astype(BF16)
            send(ty.at[row], ry.at[k - 1], s_ry + k - 1, (tile_at(row, x), o))
    for k in near:
        arrived(ry.at[k - 1], s_ry + k - 1)
        total = total + ry[k - 1].astype(F32)
    grow[...] = total
    ga[y, x] = total.astype(BF16)
    s_gy = sem_ids(NY - 1)
    s_gx = sem_ids(3 * NY)
    early = list(sent)
    sent.clear()
    gather_start(grad_at, s_gy, s_gx)
    for cp in early:
        cp.wait_send()

    gather_relay(grad_at, s_gy, s_gx, near[:4])

    grad_normed = scatter_z_sum(zs, zr, s_z)
    own_rows = pl.ds(pl.multiple_of(o * OWN_TOK, OWN_TOK), OWN_TOK)
    own_live = length > o // 2
    centred = mixed[own_rows, :]
    g = grad_normed * gain
    mean1 = jnp.sum(g, axis=-1, keepdims=True) * (1.0 / D)
    mean2 = jnp.sum(g * centred, axis=-1, keepdims=True) * (1.0 / D)
    grad_mixed = inv_s[own_rows, :] * (g - mean1 - centred * mean2)
    grad_mixed = jnp.where(own_live, grad_mixed, 0.0)
    hg[...] = grad_mixed.astype(BF16)
    s_h = sem_ids(2)
    s_ct = sem_ids(4)
    s_ch = sem_ids(1)
    send(hg, nb.at[0], s_h, (t, lax.rem(o + 1, NZ)))
    send(hg, nb.at[1], s_h + 1, (t, lax.rem(o + NZ - 1, NZ)))
    s_c4 = sem_ids(4)

    @pl.when(first_own)
    def _():
        for q in range(4):
            pltpu.make_async_remote_copy(
                src_ref=hg, dst_ref=chd, send_sem=ss.at[s_c4 + q], recv_sem=rs.at[s_ch],
                device_id=(dn_t, 2 * q + 1), device_id_type=MESH,
            ).start()

    @pl.when(odd_own)
    def _():
        q = o // 2
        pltpu.make_async_remote_copy(
            src_ref=hg, dst_ref=ct.at[q], send_sem=ss.at[s_c4], recv_sem=rs.at[s_ct + q],
            device_id=(up_t, 0), device_id_type=MESH,
        ).start()

    frame2[...] = jnp.zeros_like(frame2)
    for ch in range(CH):
        frame2[ch, 3:7, 3:11, :] = grad_mixed[:, 128 * ch : 128 * ch + 128].reshape(4, 8, 128)

    gather_relay(grad_at, s_gy, s_gx, near[4:])

    def gram_of(ks):
        for n, k in enumerate(ks):
            row = gather_row(grad_at, s_gx, k)
            gm16[n] = ga[row].astype(F32).reshape(96, HID).astype(BF16)
        g16 = gm16[0 : len(ks)].reshape(96 * len(ks), HID)
        return bdot(g16, g16, TN_DIMS)

    drain()
    gram = gram_of((0,) + near[:4])

    def put_before(block):
        rows3 = block.astype(F32)[8:32]
        for ch in range(CH):
            frame2[ch, 0:3, 3:11, :] = rows3[:, 128 * ch : 128 * ch + 128].reshape(3, 8, 128)

    def put_after(block):
        rows3 = block.astype(F32)[0:24]
        for ch in range(CH):
            frame2[ch, 7:10, 3:11, :] = rows3[:, 128 * ch : 128 * ch + 128].reshape(3, 8, 128)

    arrived(nb.at[0], s_h)
    arrived(nb.at[1], s_h + 1)

    @pl.when(first_own)
    def _():
        for q in range(4):
            arrived(ct.at[q], s_ct + q)
        prev_len = lens[dn_t]
        block = ct[0].astype(F32)
        for q in range(1, 4):
            block = jnp.where(prev_len == q + 1, ct[q].astype(F32), block)
        put_before(jnp.where(t > 0, block, 0.0))
        for q in range(4):
            pltpu.make_async_remote_copy(
                src_ref=hg, dst_ref=chd, send_sem=ss.at[s_c4 + q], recv_sem=rs.at[s_ch],
                device_id=(dn_t, 2 * q + 1), device_id_type=MESH,
            ).wait_send()

    @pl.when(jnp.logical_not(first_own))
    def _():
        put_before(nb[0])

    @pl.when(odd_own)
    def _():
        arrived(chd, s_ch)
        q = o // 2
        edge = jnp.where(t < NT - 1, chd[...].astype(F32), 0.0)
        put_after(jnp.where(length == q + 1, edge, nb[1].astype(F32)))
        pltpu.make_async_remote_copy(
            src_ref=hg, dst_ref=ct.at[q], send_sem=ss.at[s_c4], recv_sem=rs.at[s_ct + q],
            device_id=(up_t, 0), device_id_type=MESH,
        ).wait_send()

    @pl.when(jnp.logical_not(odd_own))
    def _():
        put_after(nb[1])

    def chunk2(ch, _):
        lanes = pl.ds(pl.multiple_of(ch * 128, 128), 128)
        acc = jnp.zeros((4, 8, 128), F32)
        for i in range(7):
            for j in range(7):
                w = dk[6 - i, 6 - j : 7 - j, lanes].reshape(1, 1, 128)
                acc = acc + w * frame2[ch, i : i + 4, j : j + 8, :]
        res = cot[own_rows, lanes].astype(F32) + acc.reshape(OWN_TOK, 128)
        tok_ref[1, :, lanes] = jnp.where(own_live, res, 0.0).astype(BF16)
        return 0

    lax.fori_loop(0, CH, chunk2, 0)

    gram = gram + gram_of(near[4:])
    eye = (
        lax.broadcasted_iota(jnp.int32, (HID, HID), 0) == lax.broadcasted_iota(jnp.int32, (HID, HID), 1)
    ).astype(F32)

    norm2 = jnp.sum(jnp.sum(gram * eye, axis=0, keepdims=True), axis=1, keepdims=True)
    root = lax.rsqrt(norm2 + EPS_NORM)
    gram = gram * (root * root)

    def times(a, b):
        return bdot(a.astype(BF16), b)

    def residue(a):
        a16 = a.astype(BF16)
        return (NS_B * a + NS_C * bdot(a16, a16)).astype(BF16)

    q0 = residue(gram)
    first = NS_A * gram + times(gram, q0)
    q1 = residue(NS_A * first + times(first, q0))
    ortho = grow[...] * root
    ortho = NS_A * ortho + times(ortho, q0)
    xo[c] = NS_A * ortho + times(ortho, q1)
    s_x = sem_ids(1)
    send(xo.at[c], xo.at[c], s_x, (sib, o))
    branch = scatter_z_sum(bs, br, s_b)
    own_keep = jnp.where(own_live, tissue[o // 2], 0).astype(F32)
    res = feat[own_rows, :].astype(F32) + (own_keep * scale) * branch
    tok_ref[0] = jnp.where(own_live, res, 0.0).astype(BF16)

    arrived(xo.at[1 - c], s_x)
    for m in range(2):
        muon_ref[m] = jnp.where(c == 0, xo[m, 0:12, :], xo[m, 12:24, :])

    for cp in sent + along_z:
        cp.wait_send()


SEMS = 160


def shards(features, cotangent, depth_kernel, ln_gain, weight_up, bias_up, weight_down, layer_scale, tissue, lengths):
    vmem = pl.BlockSpec(memory_space=pltpu.VMEM)
    hbm = pl.BlockSpec(memory_space=pltpu.HBM)
    block4 = (NY, NX, RB, HID)
    scratch = [
        pltpu.SMEM((NT,), jnp.int32),
        pltpu.SMEM((4,), jnp.int32),
        pltpu.VMEM((TOK, D), BF16),
        pltpu.VMEM((TOK, D), BF16),
        pltpu.VMEM((7, 7, D), F32),
        pltpu.VMEM((D,), F32),
        pltpu.VMEM((HID,), F32),
        pltpu.VMEM((D,), F32),
        pltpu.VMEM((2, 12, HID), BF16),
        pltpu.VMEM((12, HID), BF16),
        pltpu.VMEM((24, HID), F32),
        pltpu.VMEM((2,) + block4, BF16),
        pltpu.VMEM((2, NY, 96, HID), BF16),
        pltpu.VMEM((2, 24, D), BF16),
        pltpu.VMEM((2, 24, D), BF16),
        pltpu.VMEM((CH, 38, 16, 128), F32),
        pltpu.VMEM((TOK, D), F32),
        pltpu.VMEM((TOK, 1), F32),
        pltpu.VMEM((2, TOK, D), BF16),
        pltpu.VMEM((2, TOK, HID), BF16),
        pltpu.VMEM((NZ, OWN_TOK, D), BF16),
        pltpu.VMEM((NZ - 1, OWN_TOK, D), BF16),
        pltpu.VMEM((NZ, OWN_TOK, D), BF16),
        pltpu.VMEM((NZ - 1, OWN_TOK, D), BF16),
        pltpu.VMEM((TOK, D), BF16),
        pltpu.VMEM((TOK, HID), BF16),
        pltpu.VMEM(block4, F32),
        pltpu.VMEM(block4, BF16),
        pltpu.VMEM((NY, NX - 1, RB, HID), BF16),
        pltpu.VMEM((NY, RB, HID), BF16),
        pltpu.VMEM((NY - 1, RB, HID), BF16),
        pltpu.VMEM((RB, HID), F32),
        pltpu.VMEM(block4, BF16),
        pltpu.VMEM((NY, 96, HID), BF16),
        pltpu.VMEM((OWN_TOK, D), BF16),
        pltpu.VMEM((2, OWN_TOK, D), BF16),
        pltpu.VMEM((4, OWN_TOK, D), BF16),
        pltpu.VMEM((OWN_TOK, D), BF16),
        pltpu.VMEM((CH, 10, 16, 128), F32),
        pltpu.VMEM((2, RB, HID), F32),
        pltpu.SemaphoreType.DMA((SEMS,)),
        pltpu.SemaphoreType.DMA((SEMS,)),
        pltpu.SemaphoreType.DMA((10,)),
    ]
    outs = pl.pallas_call(
        body,
        out_shape=(
            jax.ShapeDtypeStruct((2, OWN_TOK, D), BF16),
            jax.ShapeDtypeStruct((2, 12, HID), F32),
        ),
        in_specs=[hbm] * 10,
        out_specs=(vmem,) * 2,
        scratch_shapes=scratch,
        compiler_params=pltpu.CompilerParams(
            collective_id=0, has_side_effects=True, vmem_limit_bytes=62 << 20
        ),
    )(
        lengths,
        tissue.reshape(4),
        features.reshape(TOK, D),
        cotangent.reshape(TOK, D),
        depth_kernel,
        ln_gain,
        weight_up,
        bias_up,
        weight_down.T,
        layer_scale,
    )
    tokens, muon = outs
    return (
        tokens[0].reshape(4, 8, D),
        tokens[1].reshape(4, 8, D),
        muon[0],
        muon[1].T,
    )


def solution(mesh):
    in_specs = (
        P("tile", None, None),
        P("tile", None, None),
        P(),
        P(),
        P("tile", "own"),
        P("own"),
        P("own", "tile"),
        P(),
        P("tile", None),
        P(),
    )
    out_specs = (
        P(("tile", "own"), None, None),
        P(("tile", "own"), None, None),
        P("tile", "own"),
        P("own", "tile"),
    )
    return jax.shard_map(shards, mesh=mesh, in_specs=in_specs, out_specs=out_specs, check_vma=False)
```
